512 devices in a mesh: seq: 8 (over z_hi, core), head: 16 (over z_lo, y), dp: 4 (over x).
Axes of the slice: x: 4, y: 8, z: 8 (z_hi: 4, z_lo: 2; z = z_hi * 2 + z_lo), core: 2. Of those that a mesh axis runs over, the one named last changes fastest.
Arguments:
- tokens: bfloat16 [4, 1024, 4096], P('dp', 'seq', 'head'), may hold values from -6 to 6
- w_qkv: bfloat16 [4096, 3, 2048], P(('seq', 'dp'), None, 'head'), may hold values from -0.09375 to 0.09375
- w_lr: bfloat16 [4096, 16], P(None, 'head'), may hold values from -0.1875 to 0.1875
- w_out: bfloat16 [4096, 2048], P(('seq', 'dp'), 'head'), may hold values from -0.125 to 0.125
- w1_init: float32 [16, 128, 512], P('head'), may hold values from -0.5 to 0.5
- w2_init: float32 [16, 512, 128], P('head'), may hold values from -0.25 to 0.25
- d_out: bfloat16 [4, 1024, 4096], P('dp', 'seq', 'head'), may hold values from -6 to 6
Outputs:
- out: bfloat16 [4, 1024, 4096], P('dp', 'seq', 'head')
- d_tokens: bfloat16 [4, 1024, 4096], P('dp', 'seq', 'head')
- d_w1_init: float32 [16, 128, 512], P('head', None, ('seq', 'dp'))
- d_w2_init: float32 [16, 512, 128], P('head', ('seq', 'dp'))
The draws below stay inside these ranges and needn't reach their ends.
All inputs are finite; a program needn't handle non-finite values.
Results may differ from the reference program's by a relative error of at most 0.018.
Values may be sent and summed in bfloat16 or wider, within the bound.
A program may use at most 64 MiB of HBM per device.

```python
import jax
import jax.numpy as jnp
from jax import lax

D = 4096
HD = 128
INNER = 512
MB = 64
HEADS = 16
BATCH = 4
LENGTH = 1024


def block_scale(rng, extent, split, least, high):
    def one(axis_at, shards_of):
        steps = jax.random.uniform(jax.random.fold_in(jax.random.fold_in(rng, 6), axis_at), (shards_of,), jnp.float32, least / len(split), high / len(split))
        return jnp.repeat(jnp.exp(steps), extent[axis_at] // shards_of).reshape((-1,) + (1,) * (len(extent) - axis_at - 1))

    factor_of = one(*split[0])
    for cut in split[1:]:
        factor_of = factor_of * one(*cut)
    return factor_of


def gaussian(own_key, shape, scale, bound, shards=(), kind=jnp.bfloat16):
    values = scale * jax.random.normal(own_key, shape, jnp.float32)
    if shards:
        values = values * block_scale(own_key, shape, shards, -0.22, 0.18)
    return jnp.clip(values, -bound, bound).astype(kind)


def setup_inputs(seed: int = 0) -> dict:
    seeds = jax.random.split(jax.random.key(seed), 8)
    tokens = gaussian(seeds[0], (BATCH, LENGTH, D), 1.0, 6.0, ((0, 4), (1, 8), (2, 16)))
    w_qkv = gaussian(seeds[1], (D, 3, HEADS * HD), D ** -0.5, 0.09375, ((0, 32), (2, 16)))
    w_lr = gaussian(seeds[2], (D, HEADS), (D // 4) ** -0.5, 0.1875, ((1, 16),))
    w_out = gaussian(seeds[3], (D, HEADS * HD), (HEADS * HD) ** -0.5, 0.125, ((0, 32), (1, 16)))
    w1_init = gaussian(seeds[4], (HEADS, HD, INNER), HD ** -0.5, 0.5, ((0, 16),), jnp.float32)
    w2_init = gaussian(seeds[5], (HEADS, INNER, HD), INNER ** -0.5, 0.25, ((0, 16),), jnp.float32)
    d_out = gaussian(seeds[6], (BATCH, LENGTH, D), 1.0, 6.0, ((0, 4), (1, 8), (2, 16)))
    return dict(tokens=tokens, w_qkv=w_qkv, w_lr=w_lr, w_out=w_out, w1_init=w1_init, w2_init=w2_init, d_out=d_out)


EPSILON = 1e-06
BASE_RATE = 0.1
GELU_SCALE = 0.7978845608028654
GELU_CUBIC = 0.044715
PRECISE = lax.Precision.HIGHEST
CONTRACT_LAST = (((1,), (1,)), ((), ()))
CONTRACT_FIRST = (((0,), (0,)), ((), ()))

def gelu_value(inputs):
    bend = jnp.tanh(GELU_SCALE * (inputs + GELU_CUBIC * inputs * inputs * inputs))
    return 0.5 * inputs * (1.0 + bend)

def gelu_slope(inputs):
    bend = jnp.tanh(GELU_SCALE * (inputs + GELU_CUBIC * inputs * inputs * inputs))
    return 0.5 * (1.0 + bend) + 0.5 * inputs * (1.0 - bend * bend) * GELU_SCALE * (1.0 + 3.0 * GELU_CUBIC * inputs * inputs)

def float_dot(left, right):
    return jnp.dot(left, right, precision=PRECISE)

def float_dims(left, right, dims):
    return lax.dot_general(left, right, dims, precision=PRECISE)

def norm_rows(inputs):
    centred = inputs - lax.optimization_barrier(jnp.mean(inputs, axis=-1, keepdims=True))
    inv_scale = lax.rsqrt(lax.optimization_barrier(jnp.mean(centred * centred, axis=-1, keepdims=True)) + EPSILON)
    return (centred * inv_scale, inv_scale)

def local_grads(w_first, w_second, key_rows, value_rows):
    pre_first = float_dot(key_rows, w_first)
    hidden = gelu_value(pre_first)
    normed, inv_scale = norm_rows(float_dot(hidden, w_second))
    residual = normed - (value_rows - key_rows)
    grad_second = inv_scale * (residual - lax.optimization_barrier(jnp.mean(residual, axis=-1, keepdims=True)) - normed * lax.optimization_barrier(jnp.mean(residual * normed, axis=-1, keepdims=True)))
    grad_first = float_dims(grad_second, w_second, CONTRACT_LAST) * gelu_slope(pre_first)
    return (hidden, grad_first, grad_second)

def inner_update(w_first, w_second, key_rows, hidden, grad_first, grad_second, rates):
    new_first = w_first - float_dims(key_rows, grad_first * rates[:, None], CONTRACT_FIRST)
    new_second = w_second - float_dims(hidden, grad_second * rates[:, None], CONTRACT_FIRST)
    return (new_first, new_second)

def inner_block(state_carry, block_rows):
    w_first, w_second = state_carry
    queries, key_rows, value_rows, rate_logit = block_rows
    rates = BASE_RATE * jax.nn.sigmoid(rate_logit) / key_rows.shape[1]
    hidden, grad_first, grad_second = local_grads(w_first, w_second, key_rows, value_rows)
    size_block = key_rows.shape[0]
    positions = lax.broadcasted_iota(jnp.int32, (size_block, size_block), 0)
    sources = lax.broadcasted_iota(jnp.int32, (size_block, size_block), 1)
    causal = jnp.where(sources <= positions, rates[None, :], jnp.float32(0.0))
    mix_first = float_dims(queries, key_rows, CONTRACT_LAST) * causal
    pre_query = float_dot(queries, w_first) - float_dot(mix_first, grad_first)
    hidden_query = gelu_value(pre_query)
    mix_second = float_dims(hidden_query, hidden, CONTRACT_LAST) * causal
    normed, unused = norm_rows(float_dot(hidden_query, w_second) - float_dot(mix_second, grad_second))
    new_state = inner_update(w_first, w_second, key_rows, hidden, grad_first, grad_second, rates)
    return (new_state, queries + normed)

def inner_run(w_first, w_second, queries, key_rows, value_rows, rate_logit):
    row_count = queries.shape[0]
    blocks = row_count // MB
    shaped = (queries.reshape(blocks, MB, -1), key_rows.reshape(blocks, MB, -1), value_rows.reshape(blocks, MB, -1), rate_logit.reshape(blocks, MB))
    final_state, outputs = lax.scan(inner_block, (w_first, w_second), shaped)
    return (final_state[0], final_state[1], outputs.reshape(row_count, -1))

def reference(tokens, w_qkv, w_lr, w_out, w1_init, w2_init, d_out):
    flat = tokens.reshape(BATCH * LENGTH, D)
    projected = jnp.dot(flat, w_qkv.reshape(D, 3 * HEADS * HD), preferred_element_type=jnp.float32)
    projected = projected.reshape(BATCH, LENGTH, 3, HEADS, HD)
    rate_logit = jnp.dot(flat, w_lr, preferred_element_type=jnp.float32).reshape(BATCH, LENGTH, HEADS)
    queries = projected[:, :, 0].transpose(0, 2, 1, 3)
    key_rows = projected[:, :, 1].transpose(0, 2, 1, 3)
    value_rows = projected[:, :, 2].transpose(0, 2, 1, 3)
    logits = rate_logit.transpose(0, 2, 1)

    def head_forward(w_first, w_second, query_h, key_h, value_h, logit_h):
        return inner_run(w_first, w_second, query_h, key_h, value_h, logit_h)[2]

    def seq_forward(inputs):
        return jax.vmap(head_forward)(w1_init, w2_init, inputs[0], inputs[1], inputs[2], inputs[3])
    ttt_heads = lax.map(seq_forward, (queries, key_rows, value_rows, logits))
    ttt_out = ttt_heads.astype(jnp.bfloat16)
    head_rows = ttt_out.transpose(1, 0, 2, 3).reshape(HEADS, BATCH * LENGTH, HD)
    out_columns = w_out.reshape(D, HEADS, HD).transpose(1, 0, 2)

    def add_out(running_sum, pieces):
        head_term = lax.dot_general(pieces[0], pieces[1], CONTRACT_LAST, preferred_element_type=jnp.float32)
        rounded = lax.optimization_barrier(head_term.astype(jnp.bfloat16))
        return (running_sum + rounded.astype(jnp.float32), None)
    out_sum, unused = lax.scan(add_out, jnp.zeros((BATCH * LENGTH, D), jnp.float32), (head_rows, out_columns))
    out = out_sum.astype(jnp.bfloat16).reshape(BATCH, LENGTH, D)
    d_flat = d_out.reshape(BATCH * LENGTH, D)
    d_ttt = jnp.dot(d_flat, w_out, preferred_element_type=jnp.float32)
    d_ttt = d_ttt.reshape(BATCH, LENGTH, HEADS, HD).transpose(0, 2, 1, 3)

    def head_backward(w_first, w_second, query_h, key_h, value_h, logit_h, cotangent_h):
        results, pull = jax.vjp(inner_run, w_first, w_second, query_h, key_h, value_h, logit_h)
        return pull((jnp.zeros_like(results[0]), jnp.zeros_like(results[1]), cotangent_h))

    def seq_backward(inputs):
        return jax.vmap(head_backward)(w1_init, w2_init, inputs[0], inputs[1], inputs[2], inputs[3], inputs[4])
    grads = lax.map(seq_backward, (queries, key_rows, value_rows, logits, d_ttt))
    d_w1_init = lax.optimization_barrier(jnp.sum(grads[0], axis=0))
    d_w2_init = lax.optimization_barrier(jnp.sum(grads[1], axis=0))
    d_proj = jnp.stack([grads[2], grads[3], grads[4]], axis=3)
    d_proj = d_proj.transpose(1, 0, 2, 3, 4).reshape(HEADS, BATCH * LENGTH, 3 * HD).astype(jnp.bfloat16)
    d_logit = grads[5].transpose(1, 0, 2).reshape(HEADS, BATCH * LENGTH)
    qkv_heads = w_qkv.reshape(D, 3, HEADS, HD).transpose(2, 0, 1, 3).reshape(HEADS, D, 3 * HD)
    rate_rows = w_lr.transpose(1, 0)

    def add_grad(running_sum, pieces):
        head_term = lax.dot_general(pieces[0], pieces[1], CONTRACT_LAST, preferred_element_type=jnp.float32)
        head_term = head_term + pieces[2][:, None] * pieces[3].astype(jnp.float32)[None, :]
        rounded = lax.optimization_barrier(head_term.astype(jnp.bfloat16))
        return (running_sum + rounded.astype(jnp.float32), None)
    grad_sum, unused = lax.scan(add_grad, jnp.zeros((BATCH * LENGTH, D), jnp.float32), (d_proj, qkv_heads, d_logit, rate_rows))
    d_tokens = grad_sum.astype(jnp.bfloat16).reshape(BATCH, LENGTH, D)
    return (out, d_tokens, d_w1_init, d_w2_init)
```

```python
import math

import jax
import jax.numpy as jnp
from jax import lax
from jax.experimental import pallas as pl
from jax.experimental.pallas import tpu as pltpu
from jax.sharding import PartitionSpec as P

MB = 64
HD = 128
BF16 = jnp.bfloat16
F32 = jnp.float32
MESH = pl.DeviceIdType.MESH
EPSILON = 1e-06
BASE_RATE = 0.1
GELU_SCALE = 0.7978845608028654
GELU_CUBIC = 0.044715
CONTRACT_LAST = (((1,), (1,)), ((), ()))
CONTRACT_FIRST = (((0,), (0,)), ((), ()))


def joined_along(parts, dim):
    parts = jnp.moveaxis(parts, 0, dim)
    lengths = parts.shape
    return parts.reshape(*lengths[:dim], lengths[dim] * lengths[dim + 1], *lengths[dim + 2 :])


def from_everyone(array, axis):
    copies = jnp.broadcast_to(array, (lax.axis_size(axis), *array.shape))
    return lax.all_to_all(copies, axis, split_axis=0, concat_axis=0, tiled=True)


def gather_directly(array, axis, dim):
    return joined_along(from_everyone(array, axis), dim)


def in_one_piece(arrays, axis, dim, along):
    widths = [math.prod(a.shape[along:]) for a in arrays]
    both = jnp.concatenate(
        [a.reshape(*a.shape[:along], w) for a, w in zip(arrays, widths)], axis=along
    )
    out = lax.all_gather(both, axis, axis=dim, tiled=True)
    parts = jnp.split(out, [sum(widths[:k]) for k in range(1, len(widths))], axis=along)
    return tuple((b.reshape(*out.shape[:along], *a.shape[along:]) for a, b in zip(arrays, parts)))


def in_blocks(array, dim, peers):
    before, after = (array.shape[:dim], array.shape[dim + 1 :])
    return jnp.moveaxis(array.reshape(*before, peers, -1, *after), dim, 0)


def summed_on_arrival(array, axis, dim):
    peers = lax.axis_size(axis)
    parts = lax.all_to_all(in_blocks(array, dim, peers), axis, 0, 0, tiled=True)
    return jnp.sum(parts.astype(jnp.float32), axis=0)


def matmul(left, right):
    return jnp.dot(left.astype(BF16), right.astype(BF16), preferred_element_type=F32)


def matmul_last(left, right):
    return lax.dot_general(left.astype(BF16), right.astype(BF16), CONTRACT_LAST, preferred_element_type=F32)


def matmul_first(left, right):
    return lax.dot_general(left.astype(BF16), right.astype(BF16), CONTRACT_FIRST, preferred_element_type=F32)


def row_mean(rows):
    return jnp.mean(rows, axis=-1, keepdims=True)


def row_sum(rows):
    return jnp.sum(rows, axis=-1, keepdims=True)


def spread(rates):
    return jnp.concatenate([rates] * 4, axis=1)


def gelu_parts(v, order):
    square = v * v
    bend = jnp.tanh(GELU_SCALE * (v + GELU_CUBIC * square * v))
    tilt = GELU_SCALE * (1.0 + 3.0 * GELU_CUBIC * square)
    flat = 1.0 - bend * bend
    half = 0.5 * v
    value = half * (1.0 + bend)
    slope = 0.5 * (1.0 + bend) + half * flat * tilt
    if order == 1:
        return value, slope
    curve = flat * (tilt + half * (6.0 * GELU_SCALE * GELU_CUBIC) * v - v * bend * tilt * tilt)
    return value, slope, curve


def norm_rows(rows):
    centred = rows - row_mean(rows)
    inv_scale = lax.rsqrt(row_mean(centred * centred) + EPSILON)
    return centred * inv_scale, inv_scale


def inner_kernel(
    q_ref, k_ref, t_ref, e_ref, chunk_ref, dt_ref, w1_ref, w2_ref,
    out_ref, dproj_ref, dlogit_ref, dw1_ref, dw2_ref,
    chunks, s1, s2, in1, in2, snd1, snd2, w1b, w2b,
    sv_wide, sv_x2, sv_narrow, sv_kt, sv_x2t, sv_eg1, b_w1, b_w2,
    chunk_send, chunk_recv, hop_send, hop_recv,
):
    place = lax.axis_index("seq")
    count = lax.axis_size("seq")
    barrier = pltpu.get_barrier_semaphore()

    def greet(step, carry):
        pl.semaphore_signal(
            barrier, inc=1, device_id={"seq": lax.rem(place + step, count)}, device_id_type=MESH
        )
        return carry

    lax.fori_loop(1, count, greet, 0)
    pl.semaphore_wait(barrier, count - 1)

    def chunk_copy(source, target):
        return pltpu.make_async_remote_copy(
            src_ref=chunk_ref,
            dst_ref=chunks.at[source],
            send_sem=chunk_send.at[target],
            recv_sem=chunk_recv.at[source],
            device_id={"seq": target},
            device_id_type=MESH,
        )

    def send_chunk(step, carry):
        chunk_copy(place, count - 1 - step).start()
        return carry

    lax.fori_loop(0, count - 1 - place, send_chunk, 0)

    s1[...] = w1_ref[...]
    s2[...] = w2_ref[...]

    def replay_block(k, t, e):
        first, second = s1[...].astype(BF16), s2[...].astype(BF16)
        x2, slope = gelu_parts(matmul(k, first), 1)
        n, s = norm_rows(matmul(x2, second))
        r = n - t
        g2 = s * (r - row_mean(r) - n * row_mean(r * n))
        g1 = matmul_last(g2, second) * slope
        s1[...] = s1[...] - matmul_first(k, spread(e) * g1)
        s2[...] = s2[...] - matmul_first(x2, e * g2)

    def replay_turn(turn, carry):
        chunk_copy(turn, place).wait_recv()
        for half in range(2):
            rows = chunks[turn, half * MB : (half + 1) * MB, :]
            replay_block(
                rows[:, :HD], rows[:, HD : 2 * HD].astype(F32), rows[:, 2 * HD :].astype(F32)
            )
        return carry

    lax.fori_loop(0, place, replay_turn, 0)

    place_row = lax.broadcasted_iota(jnp.int32, (MB, MB), 0)
    place_col = lax.broadcasted_iota(jnp.int32, (MB, MB), 1)
    for block in range(2):
        span = slice(block * MB, (block + 1) * MB)
        q, k, t, e = q_ref[span, :], k_ref[span, :], t_ref[span, :], e_ref[span, :]
        first, second = s1[...].astype(BF16), s2[...].astype(BF16)
        w1b[block] = first
        w2b[block] = second
        x2, slope, curve = gelu_parts(matmul(k, first), 2)
        n, s = norm_rows(matmul(x2, second))
        r = n - t
        cross = row_mean(r * n)
        h = r - row_mean(r) - n * cross
        g2 = s * h
        m = matmul_last(g2, second)
        g1 = m * slope
        e_wide = spread(e)
        eg1 = e_wide * g1
        eg2 = e * g2
        kt = jnp.transpose(k)
        x2t = jnp.transpose(x2)
        s1[...] = s1[...] - matmul(kt, eg1)
        s2[...] = s2[...] - matmul(x2t, eg2)

        e_row = jnp.transpose(e)[:MB, :]
        causal = jnp.where(place_col <= place_row, e_row, 0.0)
        raw1 = matmul_last(q, k)
        a1 = raw1 * causal
        zq = matmul(q, first) - matmul(a1, g1)
        xq, slope_q = gelu_parts(zq, 1)
        raw2 = matmul_last(xq, x2)
        a2 = raw2 * causal
        nq, sq = norm_rows(matmul(xq, second) - matmul(a2, g2))
        out_ref[span, :] = (q + nq).astype(BF16)
        do = dt_ref[span, :]
        dyq = sq * (do - row_mean(do) - nq * row_mean(do * nq))
        da2 = -matmul_last(dyq, g2)
        ds2 = da2 * causal
        dxq = matmul_last(dyq, second) + matmul(ds2, x2)
        dzq = dxq * slope_q
        da1 = -matmul_last(dzq, g1)
        ds1 = da1 * causal
        kept = jnp.where(place_col <= place_row, da2 * raw2 + da1 * raw1, 0.0)
        de_col = row_sum(jnp.transpose(kept))
        dproj_ref[span, :HD] = (do + matmul_last(dzq, first) + matmul(ds1, k)).astype(BF16)
        b_w1[block] = matmul_first(q, dzq)
        b_w2[block] = matmul_first(xq, dyq)
        sv_wide[block, 0] = -matmul_first(a1, dzq)
        sv_wide[block, 1] = matmul_first(ds2, xq)
        sv_wide[block, 2] = slope
        sv_wide[block, 3] = curve
        sv_wide[block, 4] = m
        sv_x2[block] = x2.astype(BF16)
        sv_eg1[block] = eg1.astype(BF16)
        sv_kt[block] = kt.astype(BF16)
        sv_x2t[block] = x2t.astype(BF16)
        sv_narrow[block, 0] = -matmul_first(a2, dyq)
        sv_narrow[block, 1] = matmul_first(ds1, q)
        sv_narrow[block, 2] = jnp.broadcast_to(de_col, (MB, HD))
        sv_narrow[block, 3] = n
        sv_narrow[block, 4] = r
        sv_narrow[block, 5] = h
        sv_narrow[block, 6] = g2
        sv_narrow[block, 7] = jnp.broadcast_to(s, (MB, HD))
        sv_narrow[block, 8] = jnp.broadcast_to(cross, (MB, HD))
        sv_narrow[block, 9] = eg2

    def hop(target, which):
        return pltpu.make_async_remote_copy(
            src_ref=(snd1, snd2)[which],
            dst_ref=(in1, in2)[which],
            send_sem=hop_send.at[which],
            recv_sem=hop_recv.at[which],
            device_id={"seq": target},
            device_id_type=MESH,
        )

    @pl.when(place == count - 1)
    def _():
        in1[...] = jnp.zeros_like(in1)
        in2[...] = jnp.zeros_like(in2)

    @pl.when(place < count - 1)
    def _():
        hop(0, 0).wait_recv()
        hop(0, 1).wait_recv()

    for block in (1, 0):
        span = slice(block * MB, (block + 1) * MB)
        if block == 1:
            d1b, d2b = in1[...], in2[...]
            d1, d2 = d1b.astype(F32), d2b.astype(F32)
        else:
            d1, d2 = dw1_ref[...], dw2_ref[...]
            d1b, d2b = d1.astype(BF16), d2.astype(BF16)
        k, e = k_ref[span, :], e_ref[span, :]
        first, second = w1b[block], w2b[block]
        b_g1, b_x2, slope, curve, m = (sv_wide[block, i] for i in range(5))
        b_g2, b_k, b_e, n, r, h, g2, s, cross, eg2 = (sv_narrow[block, i] for i in range(10))
        x2 = sv_x2[block]
        p1 = matmul(k, d1b)
        p2 = matmul(x2, d2b)
        dg1 = b_g1 - spread(e) * p1
        dm = dg1 * slope
        dmb = dm.astype(BF16)
        dg2 = b_g2 - e * p2 + matmul(dmb, second)
        dh = s * dg2
        mean_n = row_mean(dh * n)
        dr = dh - row_mean(dh) - n * mean_n
        dn = dr - cross * dh - r * mean_n
        dy = s * (dn - row_mean(dn) - n * row_mean(dn * n)) - n * (row_mean(dg2 * h) * s * s)
        dyb = dy.astype(BF16)
        dx2 = b_x2 - matmul_last(eg2, d2b) + matmul_last(dyb, second)
        dz1 = dx2 * slope + dg1 * m * curve
        dz1b = dz1.astype(BF16)
        d2 = d2 + b_w2[block] + matmul_first(dmb, g2) + matmul(sv_x2t[block], dyb)
        d1 = d1 + b_w1[block] + matmul(sv_kt[block], dz1b)
        dw1_ref[...] = d1
        dw2_ref[...] = d2
        if block == 0:
            snd1[...] = d1.astype(BF16)
            snd2[...] = d2.astype(BF16)

            @pl.when(place > 0)
            def _():
                hop(place - 1, 0).start()
                hop(place - 1, 1).start()

        dk = b_k - matmul_last(sv_eg1[block], d1b) + dr + matmul_last(dz1b, first)
        de = b_e - row_sum(p1 * m * slope) - row_sum(p2 * g2)
        dproj_ref[span, HD : 2 * HD] = dk.astype(BF16)
        dproj_ref[span, 2 * HD :] = (-dr).astype(BF16)
        dlogit_ref[span, :] = de * e * (1.0 - e * (HD / BASE_RATE))

    @pl.when(place > 0)
    def _():
        hop(place - 1, 0).wait_send()
        hop(place - 1, 1).wait_send()

    def sent_chunk(step, carry):
        chunk_copy(place, count - 1 - step).wait_send()
        return carry

    lax.fori_loop(0, count - 1 - place, sent_chunk, 0)


def inner_layer(q, k, t, e, chunk, d_ttt, w_first, w_second):
    rows = q.shape[0]
    peers = lax.axis_size("seq")
    inner = w_first.shape[1]
    vmem = pl.BlockSpec(memory_space=pltpu.VMEM)
    return pl.pallas_call(
        inner_kernel,
        out_shape=(
            jax.ShapeDtypeStruct((rows, HD), BF16),
            jax.ShapeDtypeStruct((rows, 3 * HD), BF16),
            jax.ShapeDtypeStruct((rows, HD), F32),
            jax.ShapeDtypeStruct((HD, inner), F32),
            jax.ShapeDtypeStruct((inner, HD), F32),
        ),
        in_specs=[vmem] * 8,
        out_specs=(vmem,) * 5,
        scratch_shapes=[
            pltpu.VMEM((peers, rows, 3 * HD), BF16),
            pltpu.VMEM((HD, inner), F32),
            pltpu.VMEM((inner, HD), F32),
            pltpu.VMEM((HD, inner), BF16),
            pltpu.VMEM((inner, HD), BF16),
            pltpu.VMEM((HD, inner), BF16),
            pltpu.VMEM((inner, HD), BF16),
            pltpu.VMEM((2, HD, inner), BF16),
            pltpu.VMEM((2, inner, HD), BF16),
            pltpu.VMEM((2, 5, MB, inner), F32),
            pltpu.VMEM((2, MB, inner), BF16),
            pltpu.VMEM((2, 10, MB, HD), F32),
            pltpu.VMEM((2, HD, MB), BF16),
            pltpu.VMEM((2, inner, MB), BF16),
            pltpu.VMEM((2, MB, inner), BF16),
            pltpu.VMEM((2, HD, inner), F32),
            pltpu.VMEM((2, inner, HD), F32),
            pltpu.SemaphoreType.DMA((peers,)),
            pltpu.SemaphoreType.DMA((peers,)),
            pltpu.SemaphoreType.DMA((2,)),
            pltpu.SemaphoreType.DMA((2,)),
        ],
        compiler_params=pltpu.CompilerParams(collective_id=0, has_side_effects=True),
        name="inner_layer",
    )(q, k, t, e, chunk, d_ttt, w_first, w_second)


def gradient_shares(first, second):
    peers, groups = lax.axis_size("seq"), lax.axis_size("dp")
    both = jnp.concatenate([first.transpose(1, 0), second], axis=1)
    width = both.shape[1]
    parts = both.reshape(peers, groups, -1, width).transpose(1, 0, 2, 3)
    summed = jnp.sum(lax.all_to_all(parts, "dp", 0, 0, tiled=True), axis=0)
    own = lax.all_to_all(summed, "seq", 0, 0, tiled=True)[0]
    return own[:, :HD].transpose(1, 0)[None], own[:, HD:][None]


def body(tokens, w_qkv, w_lr, w_out, w1_init, w2_init, d_out):
    head_width = w_qkv.shape[2]
    features = gather_directly(tokens[0], "head", 1)
    part_qkv, part_out = in_one_piece((w_qkv, w_out), "dp", 0, 1)
    wide_qkv, wide_out = in_one_piece((part_qkv, part_out), "seq", 0, 1)
    full_depth = wide_qkv.shape[0]
    qkv_matrix = wide_qkv.reshape(full_depth, 3 * head_width)
    projected = jnp.dot(features, qkv_matrix, preferred_element_type=F32)
    rate_logit = jnp.dot(features, w_lr, preferred_element_type=F32)
    queries = projected[:, :head_width]
    key_rows = projected[:, head_width : 2 * head_width]
    target = projected[:, 2 * head_width :] - key_rows
    rates = jnp.broadcast_to(BASE_RATE * jax.nn.sigmoid(rate_logit) / head_width, target.shape)
    chunk = jnp.concatenate([key_rows, target, rates], axis=1).astype(BF16)
    d_full = gather_directly(d_out[0], "head", 1)
    d_ttt = jnp.dot(d_full, wide_out, preferred_element_type=F32)
    ttt_out, d_proj, d_logit, d_first, d_second = inner_layer(
        queries, key_rows, target, rates, chunk, d_ttt, w1_init[0], w2_init[0]
    )
    out_term = lax.dot_general(ttt_out, wide_out, CONTRACT_LAST, preferred_element_type=F32)
    out = summed_on_arrival(out_term.astype(BF16), "head", 1).astype(BF16)[None]
    grad_term = lax.dot_general(d_proj, qkv_matrix, CONTRACT_LAST, preferred_element_type=F32)
    grad_term = grad_term + d_logit[:, :1] * w_lr[:, 0].astype(F32)[None, :]
    d_tokens = summed_on_arrival(grad_term.astype(BF16), "head", 1).astype(BF16)[None]
    share_first, share_second = gradient_shares(d_first, d_second)
    return (out, d_tokens, share_first, share_second)


def solution(mesh):
    placed = (
        P("dp", "seq", "head"),
        P(("seq", "dp"), None, "head"),
        P(None, "head"),
        P(("seq", "dp"), "head"),
        P("head", None, None),
        P("head", None, None),
        P("dp", "seq", "head"),
    )
    return jax.shard_map(
        body,
        mesh=mesh,
        in_specs=placed,
        out_specs=(
            P("dp", "seq", "head"),
            P("dp", "seq", "head"),
            P("head", None, ("seq", "dp")),
            P("head", ("seq", "dp"), None),
        ),
        check_vma=False,
    )
```

```python
import jax
import jax.numpy as jnp
from jax import lax
from jax.experimental import pallas as pl
from jax.experimental.pallas import tpu as pltpu
from jax.sharding import PartitionSpec as P

MB = 64
HD = 128
BF16 = jnp.bfloat16
F32 = jnp.float32
MESH = pl.DeviceIdType.MESH
EPSILON = 1e-06
BASE_RATE = 0.1
GELU_SCALE = 0.7978845608028654
GELU_CUBIC = 0.044715
CONTRACT_LAST = (((1,), (1,)), ((), ()))
CONTRACT_FIRST = (((0,), (0,)), ((), ()))


def matmul(left, right):
    return jnp.dot(left.astype(BF16), right.astype(BF16), preferred_element_type=F32)


def matmul_last(left, right):
    return lax.dot_general(left.astype(BF16), right.astype(BF16), CONTRACT_LAST, preferred_element_type=F32)


def matmul_first(left, right):
    return lax.dot_general(left.astype(BF16), right.astype(BF16), CONTRACT_FIRST, preferred_element_type=F32)


def row_mean(rows):
    return jnp.mean(rows, axis=-1, keepdims=True)


def row_sum(rows):
    return jnp.sum(rows, axis=-1, keepdims=True)


def spread(rates):
    return jnp.concatenate([rates] * 4, axis=1)


def gelu_parts(v, order):
    square = v * v
    bend = jnp.tanh(GELU_SCALE * (v + GELU_CUBIC * square * v))
    tilt = GELU_SCALE * (1.0 + 3.0 * GELU_CUBIC * square)
    flat = 1.0 - bend * bend
    half = 0.5 * v
    value = half * (1.0 + bend)
    slope = 0.5 * (1.0 + bend) + half * flat * tilt
    if order == 1:
        return value, slope
    curve = flat * (tilt + half * (6.0 * GELU_SCALE * GELU_CUBIC) * v - v * bend * tilt * tilt)
    return value, slope, curve


def norm_rows(rows):
    centred = rows - row_mean(rows)
    inv_scale = lax.rsqrt(row_mean(centred * centred) + EPSILON)
    return centred * inv_scale, inv_scale


def layer_kernel(
    tok_ref, wqkv_ref, wlr_ref, wout_ref, w1_ref, w2_ref, dout_ref,
    out_ref, dtok_ref, share1_ref, share2_ref,
    feat, cot, wq, wo, q_ref, k_ref, t_ref, e_ref, dt_ref, chunk_ref, ttt_ref, dproj_ref, dlogit_ref,
    dw1_ref, dw2_ref, send_out, recv_out, send_tok, recv_tok, dw_send, dw_recv, dw_sum, share,
    chunks, s1, s2, in1, in2, snd1, snd2, w1b, w2b,
    sv_wide, sv_x2, sv_narrow, sv_kt, sv_x2t, sv_eg1, b_w1, b_w2,
    near_send, feat_recv, cot_send, cot_recv, wq_recv, wq_recv_low, wo_recv, wo_recv_low,
    chunk_send, chunk_recv, hop_send, hop_recv,
    out_send, out_recv, tok_send, tok_recv, dw_sems, dw_recvs, share_send, share_recv,
):
    place, head, group = (lax.axis_index(name) for name in ("seq", "head", "dp"))
    count, heads, groups = (lax.axis_size(name) for name in ("seq", "head", "dp"))
    rows = tok_ref.shape[0]
    half = rows // 2
    barrier = pltpu.get_barrier_semaphore()

    def greet_along(name, mine, size):
        def greet(step, carry):
            peer = lax.rem(mine + step, size)
            pl.semaphore_signal(barrier, inc=1, device_id={name: peer}, device_id_type=MESH)
            return carry

        lax.fori_loop(1, size, greet, 0)

    greet_along("seq", place, count)
    greet_along("head", head, heads)
    greet_along("dp", group, groups)
    pl.semaphore_wait(barrier, count + heads + groups - 3)

    started = []

    def push(src, dst, arrival, device):
        copy = pltpu.make_async_remote_copy(
            src_ref=src,
            dst_ref=dst,
            send_sem=near_send.at[len(started)],
            recv_sem=arrival,
            device_id=device,
            device_id_type=MESH,
        )
        copy.start()
        started.append(copy)

    def arrived(dst, arrival):
        pltpu.make_async_remote_copy(
            src_ref=dst,
            dst_ref=dst,
            send_sem=near_send.at[0],
            recv_sem=arrival,
            device_id={"seq": place},
            device_id_type=MESH,
        ).wait_recv()

    ring = heads // 2
    ring_at, ring_base = lax.rem(head, ring), lax.div(head, ring) * ring
    other_base = ring - ring_base
    ring_up = {"head": ring_base + lax.rem(ring_at + 1, ring)}
    ring_down = {"head": ring_base + lax.rem(ring_at + ring - 1, ring)}

    def feat_push(block, device, src=None):
        push(feat.at[block] if src is None else src, feat.at[block], feat_recv.at[block], device)

    def feat_step(base, step):
        below = base + lax.rem(ring_at + ring - step, ring)
        arrived(feat.at[below], feat_recv.at[below])
        if step < ring // 2:
            feat_push(below, ring_up)
            above = base + lax.rem(ring_at + step, ring)
            arrived(feat.at[above], feat_recv.at[above])
            if step < ring // 2 - 1:
                feat_push(above, ring_down)

    sib = place + 1 - 2 * lax.rem(place, 2)
    sibling = {"seq": sib}
    deep = [lax.rem(place + 2 * step, count) for step in range(4)]
    sib_deep = [lax.rem(sib + 2 * step, count) for step in range(4)]
    wide = [lax.rem(group + step, groups) for step in range(4)]
    deep_up, deep_down = {"seq": deep[1]}, {"seq": deep[3]}
    wide_up, wide_down = {"dp": wide[1]}, {"dp": wide[3]}

    def wq_push(block, device, src=None):
        push(wq.at[block] if src is None else src, wq.at[block], wq_recv.at[block], device)

    def wq_relay(from_below, from_above, up, down):
        push(wq.at[from_below, :half], wq.at[from_below, :half], wq_recv.at[from_below], up)
        push(wq.at[from_above, half:], wq.at[from_above, half:], wq_recv_low.at[from_above], down)

    def wq_arrived(block):
        arrived(wq.at[block], wq_recv.at[block])

    def wq_halves_arrived(block):
        arrived(wq.at[block, :half], wq_recv.at[block])
        arrived(wq.at[block, half:], wq_recv_low.at[block])

    def wq_spread(row, src=None):
        block = row * groups + group
        wq_push(block, wide_up, src)
        wq_push(block, wide_down, src)
        wq_push(block, sibling, src)

    def wq_sides(row):
        below, above = row * groups + wide[3], row * groups + wide[1]
        wq_arrived(below)
        wq_arrived(above)
        wq_relay(below, above, wide_up, wide_down)
        wq_push(below, sibling)
        wq_push(above, sibling)

    def wq_far(row):
        block = row * groups + wide[2]
        wq_halves_arrived(block)
        wq_push(block, sibling)

    own = place * groups + group
    feat_push(head, ring_up, tok_ref)
    feat_push(head, ring_down, tok_ref)
    partner = other_base + ring_at
    feat_push(head, {"head": partner}, tok_ref)
    wq_push(own, deep_up, wqkv_ref)
    wq_push(own, deep_down, wqkv_ref)
    wq_spread(place, wqkv_ref)
    push(wout_ref, wo.at[own], wo_recv.at[own], wide_up)
    push(wout_ref, wo.at[own], wo_recv.at[own], wide_down)
    feat[head] = tok_ref[...]
    cot[head] = dout_ref[...]
    wq[own] = wqkv_ref[...]
    wo[own] = wout_ref[...]
    s1[...] = w1_ref[...]
    s2[...] = w2_ref[...]

    arrived(feat.at[partner], feat_recv.at[partner])
    feat_push(partner, ring_up)
    feat_push(partner, ring_down)
    below, above = place * groups + wide[3], place * groups + wide[1]
    arrived(wo.at[below], wo_recv.at[below])
    arrived(wo.at[above], wo_recv.at[above])
    push(wo.at[below, :half], wo.at[below, :half], wo_recv.at[below], wide_up)
    push(wo.at[above, half:], wo.at[above, half:], wo_recv_low.at[above], wide_down)
    feat_step(ring_base, 1)
    wq_sides(place)
    feat_step(other_base, 1)
    far = place * groups + wide[2]
    arrived(wo.at[far, :half], wo_recv.at[far])
    arrived(wo.at[far, half:], wo_recv_low.at[far])

    def wo_rows(row):
        return pl.ds(row * groups, groups)

    def wo_push(row, device):
        push(wo.at[wo_rows(row)], wo.at[wo_rows(row)], wo_recv.at[count * groups + row], device)

    def wo_arrived(row):
        arrived(wo.at[wo_rows(row)], wo_recv.at[count * groups + row])

    for row in (deep[3], deep[1]):
        wq_arrived(row * groups + group)
    wq_relay(deep[3] * groups + group, deep[1] * groups + group, deep_up, deep_down)
    wq_spread(deep[3])
    wq_spread(deep[1])
    wo_push(place, deep_up)
    wo_push(place, deep_down)
    wo_push(place, sibling)
    feat_step(ring_base, 2)
    feat_step(other_base, 2)
    wq_far(place)
    feat_step(ring_base, 3)
    feat_step(other_base, 3)

    def cot_copy(step, source):
        return pltpu.make_async_remote_copy(
            src_ref=dout_ref,
            dst_ref=cot.at[source],
            send_sem=cot_send.at[step],
            recv_sem=cot_recv.at[source],
            device_id={"head": lax.rem(head + step, heads)},
            device_id_type=MESH,
        )

    def cot_start(step, carry):
        cot_copy(step, head).start()
        return carry

    lax.fori_loop(1, heads, cot_start, 0)
    wq_halves_arrived(deep[2] * groups + group)
    wq_spread(deep[2])
    wq_sides(deep[3])
    wq_sides(deep[1])
    wo_arrived(deep[3])
    wo_arrived(deep[1])
    low, high = deep[3] * groups, deep[1] * groups
    pair = groups // 2
    push(wo.at[pl.ds(low, pair)], wo.at[pl.ds(low, pair)], wo_recv.at[count * groups + deep[3]], deep_up)
    push(
        wo.at[pl.ds(high + pair, pair)], wo.at[pl.ds(high + pair, pair)],
        wo_recv_low.at[count * groups + deep[1]], deep_down,
    )
    wo_push(deep[3], sibling)
    wo_push(deep[1], sibling)
    wq_sides(deep[2])
    feat_step(ring_base, 4)
    feat_step(other_base, 4)
    wq_far(deep[3])
    wq_far(deep[1])
    wq_far(deep[2])
    low = deep[2] * groups
    arrived(wo.at[pl.ds(low, pair)], wo_recv.at[count * groups + deep[2]])
    arrived(wo.at[pl.ds(low + pair, pair)], wo_recv_low.at[count * groups + deep[2]])
    wo_push(deep[2], sibling)
    for row in sib_deep:
        for column in (0, 1, 3, 2):
            wq_arrived(row * groups + wide[column])

    def depth_rows(buffer, piece):
        both = buffer[pl.ds(2 * piece, 2)]
        return both.reshape(2 * rows, both.shape[-1])

    def project(piece, carry):
        total, logit = carry
        part = feat[piece]
        total = total + jnp.dot(part, depth_rows(wq, piece), preferred_element_type=F32)
        weights = jnp.broadcast_to(wlr_ref[pl.ds(piece, 1), :], (HD, 2 * rows)).astype(BF16)
        return total, logit + matmul_last(part, weights)

    projected, logit = lax.fori_loop(
        0, heads, project, (jnp.zeros((rows, 3 * HD), F32), jnp.zeros((rows, HD), F32)), unroll=4
    )
    keys = projected[:, HD : 2 * HD]
    target = projected[:, 2 * HD :] - keys
    rates = (BASE_RATE / HD) * jax.nn.sigmoid(logit)
    chunk_ref[:, :HD] = keys.astype(BF16)
    chunk_ref[:, HD : 2 * HD] = target.astype(BF16)
    chunk_ref[:, 2 * HD :] = rates.astype(BF16)
    q_ref[...] = projected[:, :HD]
    k_ref[...] = keys
    t_ref[...] = target
    e_ref[...] = rates

    def chunk_copy(source, to):
        return pltpu.make_async_remote_copy(
            src_ref=chunk_ref,
            dst_ref=chunks.at[source],
            send_sem=chunk_send.at[to],
            recv_sem=chunk_recv.at[source],
            device_id={"seq": to},
            device_id_type=MESH,
        )

    def send_chunk(step, carry):
        chunk_copy(place, count - 1 - step).start()
        return carry

    lax.fori_loop(0, count - 1 - place, send_chunk, 0)

    def replay_block(k, t, e):
        first, second = s1[...].astype(BF16), s2[...].astype(BF16)
        x2, slope = gelu_parts(matmul(k, first), 1)
        n, s = norm_rows(matmul(x2, second))
        r = n - t
        g2 = s * (r - row_mean(r) - n * row_mean(r * n))
        g1 = matmul_last(g2, second) * slope
        s1[...] = s1[...] - matmul_first(k, spread(e) * g1)
        s2[...] = s2[...] - matmul_first(x2, e * g2)

    def replay_turn(turn, carry):
        chunk_copy(turn, place).wait_recv()
        for half in range(2):
            rows = chunks[turn, half * MB : (half + 1) * MB, :]
            replay_block(
                rows[:, :HD], rows[:, HD : 2 * HD].astype(F32), rows[:, 2 * HD :].astype(F32)
            )
        return carry

    lax.fori_loop(0, place, replay_turn, 0)

    for row in sib_deep:
        wo_arrived(row)

    def gather_cotangent(step, total):
        source = lax.rem(head + step, heads)

        @pl.when(step > 0)
        def _():
            cot_copy(0, source).wait_recv()

        return total + jnp.dot(cot[source], depth_rows(wo, source), preferred_element_type=F32)

    dt_ref[...] = lax.fori_loop(0, heads, gather_cotangent, jnp.zeros((rows, HD), F32))

    place_row = lax.broadcasted_iota(jnp.int32, (MB, MB), 0)
    place_col = lax.broadcasted_iota(jnp.int32, (MB, MB), 1)
    for block in range(2):
        span = slice(block * MB, (block + 1) * MB)
        q, k, t, e = q_ref[span, :], k_ref[span, :], t_ref[span, :], e_ref[span, :]
        first, second = s1[...].astype(BF16), s2[...].astype(BF16)
        w1b[block] = first
        w2b[block] = second
        x2, slope, curve = gelu_parts(matmul(k, first), 2)
        n, s = norm_rows(matmul(x2, second))
        r = n - t
        cross = row_mean(r * n)
        h = r - row_mean(r) - n * cross
        g2 = s * h
        m = matmul_last(g2, second)
        g1 = m * slope
        e_wide = spread(e)
        eg1 = e_wide * g1
        eg2 = e * g2
        kt = jnp.transpose(k)
        x2t = jnp.transpose(x2)
        s1[...] = s1[...] - matmul(kt, eg1)
        s2[...] = s2[...] - matmul(x2t, eg2)

        e_row = jnp.transpose(e)[:MB, :]
        causal = jnp.where(place_col <= place_row, e_row, 0.0)
        raw1 = matmul_last(q, k)
        a1 = raw1 * causal
        zq = matmul(q, first) - matmul(a1, g1)
        xq, slope_q = gelu_parts(zq, 1)
        raw2 = matmul_last(xq, x2)
        a2 = raw2 * causal
        nq, sq = norm_rows(matmul(xq, second) - matmul(a2, g2))
        ttt_ref[span, :] = (q + nq).astype(BF16)
        do = dt_ref[span, :]
        dyq = sq * (do - row_mean(do) - nq * row_mean(do * nq))
        da2 = -matmul_last(dyq, g2)
        ds2 = da2 * causal
        dxq = matmul_last(dyq, second) + matmul(ds2, x2)
        dzq = dxq * slope_q
        da1 = -matmul_last(dzq, g1)
        ds1 = da1 * causal
        kept = jnp.where(place_col <= place_row, da2 * raw2 + da1 * raw1, 0.0)
        de_col = row_sum(jnp.transpose(kept))
        dproj_ref[span, :HD] = (do + matmul_last(dzq, first) + matmul(ds1, k)).astype(BF16)
        b_w1[block] = matmul_first(q, dzq)
        b_w2[block] = matmul_first(xq, dyq)
        sv_wide[block, 0] = -matmul_first(a1, dzq)
        sv_wide[block, 1] = matmul_first(ds2, xq)
        sv_wide[block, 2] = slope
        sv_wide[block, 3] = curve
        sv_wide[block, 4] = m
        sv_x2[block] = x2.astype(BF16)
        sv_eg1[block] = eg1.astype(BF16)
        sv_kt[block] = kt.astype(BF16)
        sv_x2t[block] = x2t.astype(BF16)
        sv_narrow[block, 0] = -matmul_first(a2, dyq)
        sv_narrow[block, 1] = matmul_first(ds1, q)
        sv_narrow[block, 2] = jnp.broadcast_to(de_col, (MB, HD))
        sv_narrow[block, 3] = n
        sv_narrow[block, 4] = r
        sv_narrow[block, 5] = h
        sv_narrow[block, 6] = g2
        sv_narrow[block, 7] = jnp.broadcast_to(s, (MB, HD))
        sv_narrow[block, 8] = jnp.broadcast_to(cross, (MB, HD))
        sv_narrow[block, 9] = eg2

    def share_out(step, source):
        to = lax.rem(head + step, heads)
        return pltpu.make_async_remote_copy(
            src_ref=send_out.at[to],
            dst_ref=recv_out.at[source],
            send_sem=out_send.at[to],
            recv_sem=out_recv.at[source],
            device_id={"head": to},
            device_id_type=MESH,
        )

    def send_terms():
        def one(step, carry):
            to = lax.rem(head + step, heads)
            term = matmul_last(ttt_ref[...], depth_rows(wo, to)).astype(BF16)
            send_out[to] = term

            @pl.when(step > 1)
            def _():
                share_out(step - 1, head).start()

            return carry

        lax.fori_loop(1, heads, one, 0)
        recv_out[head] = matmul_last(ttt_ref[...], depth_rows(wo, head)).astype(BF16)
        share_out(heads - 1, head).start()

    @pl.when(place < count - 1)
    def _():
        send_terms()

    def hop(target, which):
        return pltpu.make_async_remote_copy(
            src_ref=(snd1, snd2)[which],
            dst_ref=(in1, in2)[which],
            send_sem=hop_send.at[which],
            recv_sem=hop_recv.at[which],
            device_id={"seq": target},
            device_id_type=MESH,
        )

    @pl.when(place == count - 1)
    def _():
        in1[...] = jnp.zeros_like(in1)
        in2[...] = jnp.zeros_like(in2)

    @pl.when(place < count - 1)
    def _():
        hop(0, 0).wait_recv()
        hop(0, 1).wait_recv()

    for block in (1, 0):
        span = slice(block * MB, (block + 1) * MB)
        if block == 1:
            d1b, d2b = in1[...], in2[...]
            d1, d2 = d1b.astype(F32), d2b.astype(F32)
        else:
            d1, d2 = dw1_ref[...], dw2_ref[...]
            d1b, d2b = d1.astype(BF16), d2.astype(BF16)
        k, e = k_ref[span, :], e_ref[span, :]
        first, second = w1b[block], w2b[block]
        b_g1, b_x2, slope, curve, m = (sv_wide[block, i] for i in range(5))
        b_g2, b_k, b_e, n, r, h, g2, s, cross, eg2 = (sv_narrow[block, i] for i in range(10))
        x2 = sv_x2[block]
        p1 = matmul(k, d1b)
        p2 = matmul(x2, d2b)
        dg1 = b_g1 - spread(e) * p1
        dm = dg1 * slope
        dmb = dm.astype(BF16)
        dg2 = b_g2 - e * p2 + matmul(dmb, second)
        dh = s * dg2
        mean_n = row_mean(dh * n)
        dr = dh - row_mean(dh) - n * mean_n
        dn = dr - cross * dh - r * mean_n
        dy = s * (dn - row_mean(dn) - n * row_mean(dn * n)) - n * (row_mean(dg2 * h) * s * s)
        dyb = dy.astype(BF16)
        dx2 = b_x2 - matmul_last(eg2, d2b) + matmul_last(dyb, second)
        dz1 = dx2 * slope + dg1 * m * curve
        dz1b = dz1.astype(BF16)
        d2 = d2 + b_w2[block] + matmul_first(dmb, g2) + matmul(sv_x2t[block], dyb)
        d1 = d1 + b_w1[block] + matmul(sv_kt[block], dz1b)
        dw1_ref[...] = d1
        dw2_ref[...] = d2
        if block == 0:
            snd1[...] = d1.astype(BF16)
            snd2[...] = d2.astype(BF16)

            @pl.when(place > 0)
            def _():
                hop(place - 1, 0).start()
                hop(place - 1, 1).start()

        dk = b_k - matmul_last(sv_eg1[block], d1b) + dr + matmul_last(dz1b, first)
        de = b_e - row_sum(p1 * m * slope) - row_sum(p2 * g2)
        dproj_ref[span, HD : 2 * HD] = dk.astype(BF16)
        dproj_ref[span, 2 * HD :] = (-dr).astype(BF16)
        dlogit_ref[span, :] = de * e * (1.0 - e * (HD / BASE_RATE))

    @pl.when(place == count - 1)
    def _():
        send_terms()

    def share_tok(step, source):
        to = lax.rem(head + step, heads)
        return pltpu.make_async_remote_copy(
            src_ref=send_tok.at[to],
            dst_ref=recv_tok.at[source],
            send_sem=tok_send.at[to],
            recv_sem=tok_recv.at[source],
            device_id={"head": to},
            device_id_type=MESH,
        )

    def token_term(to):
        term = matmul_last(dproj_ref[...], depth_rows(wq, to))
        d_logit = dlogit_ref[...]
        both = jnp.concatenate([d_logit, d_logit], axis=1)
        return (term + both * wlr_ref[pl.ds(to, 1), :]).astype(BF16)

    def send_token_term(step, carry):
        to = lax.rem(head + step, heads)
        send_tok[to] = token_term(to)

        @pl.when(step > 1)
        def _():
            share_tok(step - 1, head).start()

        return carry

    lax.fori_loop(1, heads, send_token_term, 0)
    recv_tok[head] = token_term(head)
    share_tok(heads - 1, head).start()

    def dw_copy(step, source):
        to = lax.rem(group + step, groups)
        return pltpu.make_async_remote_copy(
            src_ref=dw_send.at[to],
            dst_ref=dw_recv.at[source],
            send_sem=dw_sems.at[step],
            recv_sem=dw_recvs.at[source],
            device_id={"dp": to},
            device_id_type=MESH,
        )

    def share_copy(to):
        return pltpu.make_async_remote_copy(
            src_ref=dw_sum.at[to],
            dst_ref=share,
            send_sem=share_send.at[to],
            recv_sem=share_recv,
            device_id={"seq": to},
            device_id_type=MESH,
        )

    @pl.when(place == 0)
    def _():
        joined = jnp.concatenate([jnp.transpose(dw1_ref[...]), dw2_ref[...]], axis=1)
        parts = joined.reshape(count, groups, -1, 2 * HD)
        for part in range(groups):
            dw_send[part] = parts[:, part]
        for step in range(1, groups):
            dw_copy(step, group).start()
        total = dw_send[group]
        for step in range(1, groups):
            source = lax.rem(group + step, groups)
            dw_copy(step, source).wait_recv()
            total = total + dw_recv[source]
        dw_sum[...] = total
        share[...] = total[0]
        for to in range(1, count):
            share_copy(to).start()

    def sum_terms(copy, received):
        def add(step, total):
            source = lax.rem(head + step, heads)

            @pl.when(step > 0)
            def _():
                copy(0, source).wait_recv()

            return total + received[source].astype(F32)

        return lax.fori_loop(0, heads, add, jnp.zeros((rows, 2 * HD), F32)).astype(BF16)

    out_ref[...] = sum_terms(share_out, recv_out)
    dtok_ref[...] = sum_terms(share_tok, recv_tok)

    @pl.when(place > 0)
    def _():
        share_copy(0).wait_recv()

    share1_ref[...] = jnp.transpose(share[:, :HD])
    share2_ref[...] = share[:, HD:]

    @pl.when(place > 0)
    def _():
        hop(place - 1, 0).wait_send()
        hop(place - 1, 1).wait_send()

    @pl.when(place == 0)
    def _():
        for step in range(1, groups):
            dw_copy(step, group).wait_send()
        for to in range(1, count):
            share_copy(to).wait_send()

    def sent_chunk(step, carry):
        chunk_copy(place, count - 1 - step).wait_send()
        return carry

    lax.fori_loop(0, count - 1 - place, sent_chunk, 0)

    def sent_terms(step, carry):
        share_out(step, head).wait_send()
        share_tok(step, head).wait_send()
        cot_copy(step, head).wait_send()
        return carry

    lax.fori_loop(1, heads, sent_terms, 0)
    for copy in started:
        copy.wait_send()


def layer(tokens, w_qkv, w_lr, w_out, w_first, w_second, d_out):
    rows, width = tokens.shape
    peers, heads, groups = (lax.axis_size(name) for name in ("seq", "head", "dp"))
    inner = w_first.shape[1]
    share = inner // (peers * groups)
    blocks = peers * groups
    vmem = pl.BlockSpec(memory_space=pltpu.VMEM)
    dma = pltpu.SemaphoreType.DMA
    return pl.pallas_call(
        layer_kernel,
        out_shape=(
            jax.ShapeDtypeStruct((rows, width), BF16),
            jax.ShapeDtypeStruct((rows, width), BF16),
            jax.ShapeDtypeStruct((HD, share), F32),
            jax.ShapeDtypeStruct((share, HD), F32),
        ),
        in_specs=[vmem] * 7,
        out_specs=(vmem,) * 4,
        scratch_shapes=[
            pltpu.VMEM((heads, rows, width), BF16),
            pltpu.VMEM((heads, rows, width), BF16),
            pltpu.VMEM((blocks, rows, 3 * HD), BF16),
            pltpu.VMEM((blocks, rows, HD), BF16),
            pltpu.VMEM((rows, HD), F32),
            pltpu.VMEM((rows, HD), F32),
            pltpu.VMEM((rows, HD), F32),
            pltpu.VMEM((rows, HD), F32),
            pltpu.VMEM((rows, HD), F32),
            pltpu.VMEM((rows, 3 * HD), BF16),
            pltpu.VMEM((rows, HD), BF16),
            pltpu.VMEM((rows, 3 * HD), BF16),
            pltpu.VMEM((rows, HD), F32),
            pltpu.VMEM((HD, inner), F32),
            pltpu.VMEM((inner, HD), F32),
            pltpu.VMEM((heads, rows, width), BF16),
            pltpu.VMEM((heads, rows, width), BF16),
            pltpu.VMEM((heads, rows, width), BF16),
            pltpu.VMEM((heads, rows, width), BF16),
            pltpu.VMEM((groups, peers, share, 2 * HD), F32),
            pltpu.VMEM((groups, peers, share, 2 * HD), F32),
            pltpu.VMEM((peers, share, 2 * HD), F32),
            pltpu.VMEM((share, 2 * HD), F32),
            pltpu.VMEM((peers, rows, 3 * HD), BF16),
            pltpu.VMEM((HD, inner), F32),
            pltpu.VMEM((inner, HD), F32),
            pltpu.VMEM((HD, inner), BF16),
            pltpu.VMEM((inner, HD), BF16),
            pltpu.VMEM((HD, inner), BF16),
            pltpu.VMEM((inner, HD), BF16),
            pltpu.VMEM((2, HD, inner), BF16),
            pltpu.VMEM((2, inner, HD), BF16),
            pltpu.VMEM((2, 5, MB, inner), F32),
            pltpu.VMEM((2, MB, inner), BF16),
            pltpu.VMEM((2, 10, MB, HD), F32),
            pltpu.VMEM((2, HD, MB), BF16),
            pltpu.VMEM((2, inner, MB), BF16),
            pltpu.VMEM((2, MB, inner), BF16),
            pltpu.VMEM((2, HD, inner), F32),
            pltpu.VMEM((2, inner, HD), F32),
            dma((64,)),
            dma((heads,)),
            dma((heads,)),
            dma((heads,)),
            dma((blocks,)),
            dma((blocks,)),
            dma((blocks + peers,)),
            dma((blocks + peers,)),
            dma((peers,)),
            dma((peers,)),
            dma((2,)),
            dma((2,)),
            dma((heads,)),
            dma((heads,)),
            dma((heads,)),
            dma((heads,)),
            dma((groups,)),
            dma((groups,)),
            dma((peers,)),
            dma(()),
        ],
        compiler_params=pltpu.CompilerParams(collective_id=0, has_side_effects=True),
        name="layer",
    )(tokens, w_qkv, w_lr, w_out, w_first, w_second, d_out)


def body(tokens, w_qkv, w_lr, w_out, w1_init, w2_init, d_out):
    depth, parts, width = w_qkv.shape
    out, d_tokens, share_first, share_second = layer(
        tokens[0],
        w_qkv.reshape(depth, parts * width),
        w_lr.astype(F32).reshape(lax.axis_size("head"), -1),
        w_out,
        w1_init[0],
        w2_init[0],
        d_out[0],
    )
    return (out[None], d_tokens[None], share_first[None], share_second[None])


def solution(mesh):
    placed = (
        P("dp", "seq", "head"),
        P(("seq", "dp"), None, "head"),
        P(None, "head"),
        P(("seq", "dp"), "head"),
        P("head", None, None),
        P("head", None, None),
        P("dp", "seq", "head"),
    )
    return jax.shard_map(
        body,
        mesh=mesh,
        in_specs=placed,
        out_specs=(
            P("dp", "seq", "head"),
            P("dp", "seq", "head"),
            P("head", None, ("seq", "dp")),
            P("head", ("seq", "dp"), None),
        ),
        check_vma=False,
    )
```

```python
import jax
import jax.numpy as jnp
from jax import lax
from jax.experimental import pallas as pl
from jax.experimental.pallas import tpu as pltpu
from jax.sharding import PartitionSpec as P

MB = 64
HD = 128
BF16 = jnp.bfloat16
F32 = jnp.float32
MESH = pl.DeviceIdType.MESH
EPSILON = 1e-06
BASE_RATE = 0.1
GELU_SCALE = 0.7978845608028654
GELU_CUBIC = 0.044715
CONTRACT_LAST = (((1,), (1,)), ((), ()))
CONTRACT_FIRST = (((0,), (0,)), ((), ()))


def matmul(left, right):
    return jnp.dot(left.astype(BF16), right.astype(BF16), preferred_element_type=F32)


def matmul_last(left, right):
    return lax.dot_general(left.astype(BF16), right.astype(BF16), CONTRACT_LAST, preferred_element_type=F32)


def matmul_first(left, right):
    return lax.dot_general(left.astype(BF16), right.astype(BF16), CONTRACT_FIRST, preferred_element_type=F32)


def row_mean(rows):
    return jnp.mean(rows, axis=-1, keepdims=True)


def row_sum(rows):
    return jnp.sum(rows, axis=-1, keepdims=True)


def spread(rates):
    return jnp.concatenate([rates] * 4, axis=1)


def gelu_parts(v, order):
    square = v * v
    bend = jnp.tanh(GELU_SCALE * (v + GELU_CUBIC * square * v))
    tilt = GELU_SCALE * (1.0 + 3.0 * GELU_CUBIC * square)
    flat = 1.0 - bend * bend
    half = 0.5 * v
    value = half * (1.0 + bend)
    slope = 0.5 * (1.0 + bend) + half * flat * tilt
    if order == 1:
        return value, slope
    curve = flat * (tilt + half * (6.0 * GELU_SCALE * GELU_CUBIC) * v - v * bend * tilt * tilt)
    return value, slope, curve


def norm_rows(rows):
    centred = rows - row_mean(rows)
    inv_scale = lax.rsqrt(row_mean(centred * centred) + EPSILON)
    return centred * inv_scale, inv_scale


def layer_kernel(
    tok_ref, wqkv_ref, wlr_ref, wout_ref, w1_ref, w2_ref, dout_ref,
    out_ref, dtok_ref, share1_ref, share2_ref,
    feat, cot, wq, wo, ttt_ref, dproj_ref, dlogit_ref, dw1_ref, dw2_ref,
    send_out, recv_out, pair_send, pair_recv, send_tok, recv_tok, dw_send, dw_recv, dw_sum, share,
    ckt, cqo, s1, s2, w1b, w2b,
    sv_slope, sv_curve, sv_m, sv_x2, sv_narrow,
    qp_xq, qp_dy, qp_wide, qp_g2, qp_dz, qp_ds, qp_kept,
    near_send, feat_recv, cot_recv, wq_recv, wq_recv_low, wo_recv, wo_recv_low,
    chunk_send, chunk_recv, qo_send, qo_recv,
    out_send, out_recv, pair_sends, pair_recvs, tok_send, tok_recv, dw_sems, dw_recvs, share_send, share_recv,
):
    place, head, group = (lax.axis_index(name) for name in ("seq", "head", "dp"))
    count, heads, groups = (lax.axis_size(name) for name in ("seq", "head", "dp"))
    rows = tok_ref.shape[0]
    half = rows // 2
    blocks = count * groups
    barrier = pltpu.get_barrier_semaphore()

    def greet_along(name, mine, size):
        def greet(step, carry):
            peer = lax.rem(mine + step, size)
            pl.semaphore_signal(barrier, inc=1, device_id={name: peer}, device_id_type=MESH)
            return carry

        lax.fori_loop(1, size, greet, 0)

    greet_along("seq", place, count)
    greet_along("head", head, heads)
    greet_along("dp", group, groups)
    pl.semaphore_wait(barrier, count + heads + groups - 3)

    started = []

    def push(src, dst, arrival, device):
        copy = pltpu.make_async_remote_copy(
            src_ref=src,
            dst_ref=dst,
            send_sem=near_send.at[len(started)],
            recv_sem=arrival,
            device_id=device,
            device_id_type=MESH,
        )
        copy.start()
        started.append(tuple(src.shape))

    def arrived(dst, arrival):
        pltpu.make_async_remote_copy(
            src_ref=dst,
            dst_ref=dst,
            send_sem=near_send.at[0],
            recv_sem=arrival,
            device_id={"seq": place},
            device_id_type=MESH,
        ).wait_recv()

    ring = heads // 2
    ring_at, ring_base = lax.rem(head, ring), lax.div(head, ring) * ring
    other_base = ring - ring_base
    partner = {"head": other_base + ring_at}
    ring_up = {"head": ring_base + lax.rem(ring_at + 1, ring)}
    ring_down = {"head": ring_base + lax.rem(ring_at + ring - 1, ring)}

    def ring_push(buffer, arrivals, block, device, src=None):
        push(buffer.at[block] if src is None else src, buffer.at[block], arrivals.at[block], device)

    def ring_start(buffer, arrivals, src):
        ring_push(buffer, arrivals, head, ring_up, src)
        ring_push(buffer, arrivals, head, ring_down, src)
        ring_push(buffer, arrivals, head, partner, src)

    def ring_partner(buffer, arrivals):
        block = other_base + ring_at
        arrived(buffer.at[block], arrivals.at[block])
        ring_push(buffer, arrivals, block, ring_up)
        ring_push(buffer, arrivals, block, ring_down)

    def ring_step(buffer, arrivals, base, step):
        below = base + lax.rem(ring_at + ring - step, ring)
        arrived(buffer.at[below], arrivals.at[below])
        if step < ring // 2:
            ring_push(buffer, arrivals, below, ring_up)
            above = base + lax.rem(ring_at + step, ring)
            arrived(buffer.at[above], arrivals.at[above])
            if step < ring // 2 - 1:
                ring_push(buffer, arrivals, above, ring_down)

    def feat_step(base, step):
        ring_step(feat, feat_recv, base, step)

    def cot_step(base, step):
        ring_step(cot, cot_recv, base, step)

    sib = place + 1 - 2 * lax.rem(place, 2)
    sibling = {"seq": sib}
    deep = [lax.rem(place + 2 * step, count) for step in range(4)]
    sib_deep = [lax.rem(sib + 2 * step, count) for step in range(4)]
    wide = [lax.rem(group + step, groups) for step in range(4)]
    deep_up, deep_down = {"seq": deep[1]}, {"seq": deep[3]}
    wide_up, wide_down = {"dp": wide[1]}, {"dp": wide[3]}

    def wq_push(block, device, src=None):
        push(wq.at[block] if src is None else src, wq.at[block], wq_recv.at[block], device)

    def wq_relay(from_below, from_above, up, down):
        push(wq.at[from_below, :half], wq.at[from_below, :half], wq_recv.at[from_below], up)
        push(wq.at[from_above, half:], wq.at[from_above, half:], wq_recv_low.at[from_above], down)

    def wq_arrived(block):
        arrived(wq.at[block], wq_recv.at[block])

    def wq_halves_arrived(block):
        arrived(wq.at[block, :half], wq_recv.at[block])
        arrived(wq.at[block, half:], wq_recv_low.at[block])

    def wq_spread(row, src=None):
        block = row * groups + group
        wq_push(block, wide_up, src)
        wq_push(block, wide_down, src)
        wq_push(block, sibling, src)

    def wq_sides(row):
        below, above = row * groups + wide[3], row * groups + wide[1]
        wq_arrived(below)
        wq_arrived(above)
        wq_relay(below, above, wide_up, wide_down)
        wq_push(below, sibling)
        wq_push(above, sibling)

    def wq_far(row):
        block = row * groups + wide[2]
        wq_halves_arrived(block)
        wq_push(block, sibling)

    layers = count // 2

    def halved(number):
        if isinstance(number, int):
            return number // 2, number % 2
        return lax.div(number, 2), lax.rem(number, 2)

    def wo_block(row, column):
        layer, side = halved(row)
        return (side * groups + column) * layers + layer

    def wo_column(row, column):
        return pl.ds((lax.rem(row, 2) * groups + column) * layers, layers)

    def wo_relay(from_below, from_above, up, down):
        push(wo.at[from_below, :half], wo.at[from_below, :half], wo_recv.at[from_below], up)
        push(wo.at[from_above, half:], wo.at[from_above, half:], wo_recv_low.at[from_above], down)

    def wo_column_push(column, device):
        at = wo_column(place, column)
        push(wo.at[at], wo.at[at], wo_recv.at[blocks + lax.rem(place, 2) * groups + column], device)

    def wo_column_arrived(row, column):
        at = wo_column(row, column)
        arrived(wo.at[at], wo_recv.at[blocks + lax.rem(row, 2) * groups + column])

    def wo_sides():
        wo_column_arrived(place, wide[3])
        wo_column_arrived(place, wide[1])
        pair = layers // 2
        low = (lax.rem(place, 2) * groups + wide[3]) * layers
        high = (lax.rem(place, 2) * groups + wide[1]) * layers + pair
        flag = blocks + lax.rem(place, 2) * groups
        push(wo.at[pl.ds(low, pair)], wo.at[pl.ds(low, pair)], wo_recv.at[flag + wide[3]], wide_up)
        push(wo.at[pl.ds(high, pair)], wo.at[pl.ds(high, pair)], wo_recv_low.at[flag + wide[1]], wide_down)
        wo_column_push(wide[3], sibling)
        wo_column_push(wide[1], sibling)

    def wo_far():
        pair = layers // 2
        low = (lax.rem(place, 2) * groups + wide[2]) * layers
        flag = blocks + lax.rem(place, 2) * groups
        arrived(wo.at[pl.ds(low, pair)], wo_recv.at[flag + wide[2]])
        arrived(wo.at[pl.ds(low + pair, pair)], wo_recv_low.at[flag + wide[2]])
        wo_column_push(wide[2], sibling)

    own = place * groups + group
    own_wo = wo_block(place, group)
    ring_start(feat, feat_recv, tok_ref)
    for part in range(3):
        wq[own, :, part * HD : (part + 1) * HD] = wqkv_ref[:, part, :]
    wq_push(own, deep_up)
    wq_push(own, deep_down)
    wq_spread(place)
    push(wout_ref, wo.at[own_wo], wo_recv.at[own_wo], deep_up)
    push(wout_ref, wo.at[own_wo], wo_recv.at[own_wo], deep_down)
    feat[head] = tok_ref[...]
    cot[head] = dout_ref[...]
    wo[own_wo] = wout_ref[...]
    feat_step(ring_base, 1)
    wq_sides(place)
    ring_partner(feat, feat_recv)
    feat_step(ring_base, 2)
    for row in (deep[3], deep[1]):
        wq_arrived(row * groups + group)
    wq_relay(deep[3] * groups + group, deep[1] * groups + group, deep_up, deep_down)
    wq_spread(deep[3])
    wq_spread(deep[1])
    wq_far(place)
    feat_step(other_base, 1)
    feat_step(ring_base, 3)
    for row in (deep[3], deep[1]):
        arrived(wo.at[wo_block(row, group)], wo_recv.at[wo_block(row, group)])
    wo_relay(wo_block(deep[3], group), wo_block(deep[1], group), deep_up, deep_down)
    feat_step(other_base, 2)
    wq_halves_arrived(deep[2] * groups + group)
    wq_spread(deep[2])
    wq_sides(deep[3])
    wq_sides(deep[1])
    feat_step(ring_base, 4)
    feat_step(other_base, 3)
    ring_start(cot, cot_recv, dout_ref)
    far = wo_block(deep[2], group)
    arrived(wo.at[far, :half], wo_recv.at[far])
    arrived(wo.at[far, half:], wo_recv_low.at[far])
    wq_sides(deep[2])
    wo_column_push(group, wide_up)
    wo_column_push(group, wide_down)
    wo_column_push(group, sibling)
    feat_step(other_base, 4)
    wq_far(deep[3])
    wq_far(deep[1])
    cot_step(ring_base, 1)
    wq_far(deep[2])
    for row in sib_deep:
        for column in (0, 1, 3, 2):
            wq_arrived(row * groups + wide[column])

    def depth_rows(buffer, piece):
        both = buffer[pl.ds(2 * piece, 2)]
        return both.reshape(2 * rows, both.shape[-1])

    def out_rows(piece):
        row, column = halved(piece)
        at = wo_block(row, 2 * column)
        return jnp.concatenate([wo[at], wo[at + layers]], axis=0)

    def rate_weights(piece):
        return jnp.concatenate([wlr_ref[pl.ds(2 * piece, 1), :], wlr_ref[pl.ds(2 * piece + 1, 1), :]], axis=1)

    def project(piece, carry):
        total, logit = carry
        part = feat[piece]
        total = total + jnp.dot(part, depth_rows(wq, piece), preferred_element_type=F32)
        weights = jnp.broadcast_to(rate_weights(piece), (HD, 2 * rows)).astype(BF16)
        return total, logit + matmul_last(part, weights)

    projected, logit = lax.fori_loop(
        0, heads, project, (jnp.zeros((rows, 3 * HD), F32), jnp.zeros((rows, HD), F32)), unroll=4
    )
    keys = projected[:, HD : 2 * HD]
    rates = (BASE_RATE / HD) * jax.nn.sigmoid(logit)
    rate_rows = jnp.transpose(rates)[:16, :]
    rate_high = rate_rows.astype(BF16)
    block_rows = ckt.at[place]
    block_rows[:rows, :HD] = keys.astype(BF16)
    block_rows[:rows, HD:] = (projected[:, 2 * HD :] - keys).astype(BF16)
    block_rows[rows:, :HD] = rate_high
    block_rows[rows:, HD:] = (rate_rows - rate_high.astype(F32)).astype(BF16)
    cqo[place, :, :HD] = projected[:, :HD].astype(BF16)

    def chunk_copy(source, to, which):
        return pltpu.make_async_remote_copy(
            src_ref=ckt.at[source],
            dst_ref=ckt.at[source],
            send_sem=chunk_send.at[which],
            recv_sem=chunk_recv.at[source],
            device_id={"seq": to},
            device_id_type=MESH,
        )

    s1[...] = w1_ref[...]
    s2[...] = w2_ref[...]
    chunk_copy(place, deep[1], count).start()
    chunk_copy(place, deep[3], count + 1).start()
    chunk_copy(place, sib, count + 2).start()
    chunk_copy(place, deep[2], count + 3).start()

    def same_side(source):
        return jnp.logical_and(source != place, lax.rem(source + place, 2) == 0)

    def take_chunk(source):
        @pl.when(source != place)
        def _():
            chunk_copy(source, place, 0).wait_recv()

        @pl.when(same_side(source))
        def _():
            chunk_copy(source, sib, source).start()

    place_row = lax.broadcasted_iota(jnp.int32, (MB, MB), 0)
    place_col = lax.broadcasted_iota(jnp.int32, (MB, MB), 1)

    def span_of(half_at):
        return slice(half_at * MB, (half_at + 1) * MB)

    def state_block(turn, half_at, e):
        block = 2 * turn + half_at
        k = ckt[turn, span_of(half_at), :HD]
        t = ckt[turn, span_of(half_at), HD:].astype(F32)
        first, second = s1[...].astype(BF16), s2[...].astype(BF16)
        x2, slope, curve = gelu_parts(matmul(k, first), 2)
        n, s = norm_rows(matmul(x2, second))
        r = n - t
        cross = row_mean(r * n)
        h = r - row_mean(r) - n * cross
        g2 = s * h
        m = matmul_last(g2, second)
        kt = jnp.transpose(k)
        x2t = jnp.transpose(x2)
        s1[...] = s1[...] - matmul(kt, spread(e) * (m * slope))
        s2[...] = s2[...] - matmul(x2t, e * g2)
        w1b[block] = first
        w2b[block] = second
        sv_slope[block] = slope
        sv_curve[block] = curve
        sv_m[block] = m
        sv_x2[block] = x2.astype(BF16)
        sv_narrow[block, 0] = n
        sv_narrow[block, 1] = r
        sv_narrow[block, 2] = h
        sv_narrow[block, 3] = g2
        sv_narrow[block, 4] = jnp.broadcast_to(s, (MB, HD))
        sv_narrow[block, 5] = jnp.broadcast_to(cross, (MB, HD))
        sv_narrow[block, 6] = e

    def query_forward(turn, half_at):
        block = 2 * turn + half_at
        span = span_of(half_at)
        q, k = cqo[turn, span, :HD], ckt[turn, span, :HD]
        first, second, x2 = w1b[block], w2b[block], sv_x2[block]
        g1 = (sv_m[block] * sv_slope[block]).astype(BF16)
        g2 = sv_narrow[block, 3].astype(BF16)
        e_row = jnp.transpose(sv_narrow[block, 6])[:MB, :]
        causal = jnp.where(place_col <= place_row, e_row, 0.0)
        raw1 = matmul_last(q, k)
        a1 = raw1 * causal
        xq, slope_q = gelu_parts(matmul(q, first) - matmul(a1, g1), 1)
        raw2 = matmul_last(xq, x2)
        a2 = raw2 * causal
        nq, sq = norm_rows(matmul(xq, second) - matmul(a2, g2))
        return q, first, second, x2, g1, g2, causal, raw1, a1, xq, slope_q, raw2, a2, nq, sq

    def query_part(turn, half_at):
        q, first, second, x2, g1, g2, causal, raw1, a1, xq, slope_q, raw2, a2, nq, sq = query_forward(
            turn, half_at
        )
        do = cqo[turn, span_of(half_at), HD:].astype(F32)
        dyq = (sq * (do - row_mean(do) - nq * row_mean(do * nq))).astype(BF16)
        da2 = -matmul_last(dyq, g2)
        ds2 = (da2 * causal).astype(BF16)
        dzq = ((matmul_last(dyq, second) + matmul(ds2, x2)) * slope_q).astype(BF16)
        da1 = -matmul_last(dzq, g1)
        qp_xq[half_at] = xq.astype(BF16)
        qp_dy[half_at] = dyq
        qp_wide[half_at, 0] = -matmul_first(a1, dzq)
        qp_wide[half_at, 1] = matmul_first(ds2, xq)
        qp_g2[half_at] = -matmul_first(a2, dyq)
        qp_dz[half_at] = dzq
        qp_ds[half_at] = (da1 * causal).astype(BF16)
        qp_kept[half_at] = jnp.where(place_col <= place_row, da2 * raw2 + da1 * raw1, 0.0)

    def chain_block(turn, half_at, mine):
        block = 2 * turn + half_at
        span = span_of(half_at)
        d1, d2 = dw1_ref[...], dw2_ref[...]
        d1b, d2b = d1.astype(BF16), d2.astype(BF16)
        k = ckt[turn, span, :HD]
        first, second, x2 = w1b[block], w2b[block], sv_x2[block]
        slope, curve, m = sv_slope[block], sv_curve[block], sv_m[block]
        n, r, h, g2, s, cross, e = (sv_narrow[block, i] for i in range(7))
        p1 = matmul(k, d1b)
        p2 = matmul_last(x2, d2b)
        dg1 = qp_wide[half_at, 0] - spread(e) * p1
        dmb = (dg1 * slope).astype(BF16)
        dg2 = qp_g2[half_at] - e * p2 + matmul(dmb, second)
        dh = s * dg2
        mean_n = row_mean(dh * n)
        dr = dh - row_mean(dh) - n * mean_n
        dn = dr - cross * dh - r * mean_n
        dy = s * (dn - row_mean(dn) - n * row_mean(dn * n)) - n * (row_mean(dg2 * h) * s * s)
        dyb = dy.astype(BF16)
        dx2 = qp_wide[half_at, 1] - matmul(e * g2, d2b) + matmul_last(dyb, second)
        dz1 = dx2 * slope + dg1 * m * curve
        dz1b = dz1.astype(BF16)
        narrow = jnp.concatenate([g2.astype(BF16), dyb, qp_dy[half_at]], axis=0)
        dw2_ref[...] = d2 + matmul_first(narrow, jnp.concatenate([dmb, x2, qp_xq[half_at]], axis=0))
        inputs = jnp.concatenate([k, cqo[turn, span, :HD]], axis=0)
        dw1_ref[...] = d1 + matmul_first(inputs, jnp.concatenate([dz1b, qp_dz[half_at]], axis=0))
        if mine:
            q, do = cqo[turn, span, :HD], cqo[turn, span, HD:].astype(F32)
            ds1 = qp_ds[half_at]
            dq = do + matmul_last(qp_dz[half_at], first) + matmul(ds1, k)
            g1 = m * slope
            dk = matmul_first(ds1, q) - matmul_last(spread(e) * g1, d1b) + dr + matmul_last(dz1b, first)
            de = row_sum(jnp.transpose(qp_kept[half_at])) - row_sum(p1 * g1) - row_sum(p2 * g2)
            dproj_ref[span, :HD] = dq.astype(BF16)
            dproj_ref[span, HD : 2 * HD] = dk.astype(BF16)
            dproj_ref[span, 2 * HD :] = (-dr).astype(BF16)
            dlogit_ref[span, :] = de * e * (1.0 - e * (HD / BASE_RATE))

    def share_out(step, source):
        to = lax.rem(head + step, heads)
        return pltpu.make_async_remote_copy(
            src_ref=send_out.at[to],
            dst_ref=recv_out.at[source],
            send_sem=out_send.at[to],
            recv_sem=out_recv.at[source],
            device_id={"head": to},
            device_id_type=MESH,
        )

    def send_terms():
        rows_out = ttt_ref[...]
        for step in range(1, heads):
            to = lax.rem(head + step, heads)
            send_out[to] = matmul_last(rows_out, out_rows(to)).astype(BF16)
            if step > 1:
                share_out(step - 1, head).start()
        recv_out[head] = matmul_last(rows_out, out_rows(head)).astype(BF16)
        share_out(heads - 1, head).start()

    def state_turn(turn, carry):
        @pl.when(turn + 2 < count)
        def _():
            take_chunk(turn + 2)

        rate_row = ckt[turn, rows:, :HD].astype(F32) + ckt[turn, rows:, HD:].astype(F32)
        spread_rates = jnp.transpose(jnp.broadcast_to(rate_row[:1, :], (HD, rows)))
        state_block(turn, 0, spread_rates[:MB])
        state_block(turn, 1, spread_rates[MB:])
        return carry

    def early_turn(turn, carry):
        state_turn(turn, 0)

        @pl.when(turn == 0)
        def _():
            ring_partner(cot, cot_recv)
            cot_step(ring_base, 2)
            wo_sides()

        @pl.when(turn == 1)
        def _():
            cot_step(other_base, 1)
            cot_step(ring_base, 3)
            wo_far()

        @pl.when(turn == 2)
        def _():
            cot_step(other_base, 2)
            cot_step(ring_base, 4)

        return carry

    def qo_copy(source, to):
        return pltpu.make_async_remote_copy(
            src_ref=cqo.at[source],
            dst_ref=cqo.at[source],
            send_sem=qo_send.at[to],
            recv_sem=qo_recv.at[source],
            device_id={"seq": to},
            device_id_type=MESH,
        )

    def late_turn(turn, carry):
        state_turn(turn, 0)

        @pl.when(turn == jnp.maximum(place, 3))
        def _():
            for half_at in range(2):
                parts = query_forward(place, half_at)
                ttt_ref[span_of(half_at), :] = (parts[0].astype(F32) + parts[-2]).astype(BF16)
            send_terms()

        @pl.when(turn == 3)
        def _():
            cot_step(other_base, 3)

        @pl.when(turn == 4)
        def _():
            cot_step(other_base, 4)
            d_ttt = jnp.zeros((rows, HD), F32)
            for piece in range(heads):
                d_ttt = d_ttt + jnp.dot(cot[piece], out_rows(piece), preferred_element_type=F32)
            cqo[place, :, HD:] = d_ttt.astype(BF16)

            def send_qo(to, carry):
                qo_copy(place, to).start()
                return carry

            lax.fori_loop(0, place, send_qo, 0)

        return carry

    take_chunk(0)
    take_chunk(1)
    lax.fori_loop(0, 3, early_turn, 0)
    for column in range(groups):
        wo_column_arrived(sib, column)
    lax.fori_loop(3, count, late_turn, 0)

    dw1_ref[...] = jnp.zeros_like(dw1_ref)
    dw2_ref[...] = jnp.zeros_like(dw2_ref)

    def take_qo(source):
        @pl.when(source > place)
        def _():
            qo_copy(source, place).wait_recv()

    take_qo(count - 1)
    query_part(count - 1, 1)

    def back_turn(step, carry):
        turn = count - 1 - step
        take_qo(turn - 1)
        chain_block(turn, 1, False)
        query_part(turn, 0)
        chain_block(turn, 0, False)
        query_part(turn - 1, 1)
        return carry

    lax.fori_loop(0, count - 1 - place, back_turn, 0)
    chain_block(place, 1, True)
    query_part(place, 0)
    chain_block(place, 0, True)

    def pair_copy(spot):
        return pltpu.make_async_remote_copy(
            src_ref=pair_send.at[spot],
            dst_ref=pair_recv.at[spot],
            send_sem=pair_sends.at[spot],
            recv_sem=pair_recvs.at[spot],
            device_id=partner,
            device_id_type=MESH,
        )

    def share_tok(spot, source):
        return pltpu.make_async_remote_copy(
            src_ref=send_tok.at[spot],
            dst_ref=recv_tok.at[source],
            send_sem=tok_send.at[spot],
            recv_sem=tok_recv.at[source],
            device_id={"head": ring_base + spot},
            device_id_type=MESH,
        )

    d_proj = dproj_ref[...]
    d_logit = jnp.concatenate([dlogit_ref[...], dlogit_ref[...]], axis=1)

    def token_term(to):
        return matmul_last(d_proj, depth_rows(wq, to)) + d_logit * rate_weights(to)

    spots = [lax.rem(ring_at + step, ring) for step in (4, 3, 5, 2, 6, 1, 7, 0)]
    for at, spot in enumerate(spots):
        pair_send[spot] = token_term(other_base + spot).astype(BF16)
        if at > 0:
            pair_copy(spots[at - 1]).start()
    last_pair = spots[-1]

    def dw_copy(step, source):
        to = lax.rem(group + step, groups)
        return pltpu.make_async_remote_copy(
            src_ref=dw_send.at[to],
            dst_ref=dw_recv.at[source],
            send_sem=dw_sems.at[step],
            recv_sem=dw_recvs.at[source],
            device_id={"dp": to},
            device_id_type=MESH,
        )

    def share_copy(to):
        return pltpu.make_async_remote_copy(
            src_ref=dw_sum.at[to],
            dst_ref=share,
            send_sem=share_send.at[to],
            recv_sem=share_recv,
            device_id={"seq": to},
            device_id_type=MESH,
        )

    @pl.when(place == 0)
    def _():
        joined = jnp.transpose(jnp.concatenate([dw1_ref[...], dw2_ref[...]], axis=0))
        parts = joined.reshape(count, groups, -1, 2 * HD)
        for part in range(groups):
            dw_send[part] = parts[:, part]
        for step in range(1, groups):
            dw_copy(step, group).start()

    for at, spot in enumerate(spots):
        term = token_term(ring_base + spot)
        if at == 0:
            pair_copy(last_pair).start()
        if at > 0:
            share_tok(spots[at - 1], ring_at).start()
        pair_copy(spot).wait_recv()
        term = (term + pair_recv[spot].astype(F32)).astype(BF16)
        if at < ring - 1:
            send_tok[spot] = term
        else:
            recv_tok[ring_at] = term

    @pl.when(place == 0)
    def _():
        total = dw_send[group]
        for step in range(1, groups):
            source = lax.rem(group + step, groups)
            dw_copy(step, source).wait_recv()
            total = total + dw_recv[source]
        dw_sum[...] = total
        share[...] = total[0]
        for to in range(1, count):
            share_copy(to).start()

    def sum_terms(copy, received):
        def add(step, total):
            source = lax.rem(head + step, heads)

            @pl.when(step > 0)
            def _():
                copy(0, source).wait_recv()

            return total + received[source].astype(F32)

        return lax.fori_loop(0, heads, add, jnp.zeros((rows, 2 * HD), F32)).astype(BF16)

    out_ref[...] = sum_terms(share_out, recv_out)
    total = recv_tok[ring_at].astype(F32)
    for step in (1, 7, 2, 6, 3, 5, 4):
        source = lax.rem(ring_at + step, ring)
        share_tok(ring_at, source).wait_recv()
        total = total + recv_tok[source].astype(F32)
    dtok_ref[...] = total.astype(BF16)

    @pl.when(place > 0)
    def _():
        share_copy(0).wait_recv()

    share1_ref[...] = share[:, :HD]
    share2_ref[...] = share[:, HD:]

    @pl.when(place == 0)
    def _():
        for step in range(1, groups):
            dw_copy(step, group).wait_send()
        for to in range(1, count):
            share_copy(to).wait_send()

    for which in range(4):
        chunk_copy(place, sib, count + which).wait_send()

    def sent_chunk(source, carry):
        @pl.when(same_side(source))
        def _():
            chunk_copy(source, sib, source).wait_send()

        return carry

    lax.fori_loop(0, count, sent_chunk, 0)

    def sent_qo(to, carry):
        qo_copy(place, to).wait_send()
        return carry

    lax.fori_loop(0, place, sent_qo, 0)

    def sent_terms(step, carry):
        share_out(step, head).wait_send()
        return carry

    lax.fori_loop(1, heads, sent_terms, 0)
    for spot in spots:
        pair_copy(spot).wait_send()
    for spot in spots[:-1]:
        share_tok(spot, ring_at).wait_send()
    views = [feat.at[0], wq.at[0], wq.at[0, :half], wo.at[0], wo.at[0, :half]]
    views += [wo.at[pl.ds(0, layers)], wo.at[pl.ds(0, layers // 2)]]
    view_of = {tuple(view.shape): view for view in views}
    for index, shape in enumerate(started):
        pltpu.make_async_remote_copy(
            src_ref=view_of[shape],
            dst_ref=view_of[shape],
            send_sem=near_send.at[index],
            recv_sem=feat_recv.at[0],
            device_id={"seq": place},
            device_id_type=MESH,
        ).wait_send()


def layer(tokens, w_qkv, w_lr, w_out, w_first, w_second, d_out):
    rows, width = tokens.shape
    peers, heads, groups = (lax.axis_size(name) for name in ("seq", "head", "dp"))
    inner = w_first.shape[1]
    share = inner // (peers * groups)
    blocks = peers * groups
    steps = peers * (rows // MB)
    vmem = pl.BlockSpec(memory_space=pltpu.VMEM)
    dma = pltpu.SemaphoreType.DMA
    return pl.pallas_call(
        layer_kernel,
        out_shape=(
            jax.ShapeDtypeStruct((rows, width), BF16),
            jax.ShapeDtypeStruct((rows, width), BF16),
            jax.ShapeDtypeStruct((share, HD), F32),
            jax.ShapeDtypeStruct((share, HD), F32),
        ),
        in_specs=[vmem] * 7,
        out_specs=(vmem,) * 4,
        scratch_shapes=[
            pltpu.VMEM((heads, rows, width), BF16),
            pltpu.VMEM((heads, rows, width), BF16),
            pltpu.VMEM((blocks, rows, 3 * HD), BF16),
            pltpu.VMEM((blocks, rows, HD), BF16),
            pltpu.VMEM((rows, HD), BF16),
            pltpu.VMEM((rows, 3 * HD), BF16),
            pltpu.VMEM((rows, HD), F32),
            pltpu.VMEM((HD, inner), F32),
            pltpu.VMEM((HD, inner), F32),
            pltpu.VMEM((heads, rows, width), BF16),
            pltpu.VMEM((heads, rows, width), BF16),
            pltpu.VMEM((heads // 2, rows, width), BF16),
            pltpu.VMEM((heads // 2, rows, width), BF16),
            pltpu.VMEM((heads // 2, rows, width), BF16),
            pltpu.VMEM((heads // 2, rows, width), BF16),
            pltpu.VMEM((groups, peers, share, 2 * HD), F32),
            pltpu.VMEM((groups, peers, share, 2 * HD), F32),
            pltpu.VMEM((peers, share, 2 * HD), F32),
            pltpu.VMEM((share, 2 * HD), F32),
            pltpu.VMEM((peers, rows + 16, 2 * HD), BF16),
            pltpu.VMEM((peers, rows, 2 * HD), BF16),
            pltpu.VMEM((HD, inner), F32),
            pltpu.VMEM((inner, HD), F32),
            pltpu.VMEM((steps, HD, inner), BF16),
            pltpu.VMEM((steps, inner, HD), BF16),
            pltpu.VMEM((steps, MB, inner), F32),
            pltpu.VMEM((steps, MB, inner), F32),
            pltpu.VMEM((steps, MB, inner), F32),
            pltpu.VMEM((steps, MB, inner), BF16),
            pltpu.VMEM((steps, 7, MB, HD), F32),
            pltpu.VMEM((2, MB, inner), BF16),
            pltpu.VMEM((2, MB, HD), BF16),
            pltpu.VMEM((2, 2, MB, inner), F32),
            pltpu.VMEM((2, MB, HD), F32),
            pltpu.VMEM((2, MB, inner), BF16),
            pltpu.VMEM((2, MB, MB), BF16),
            pltpu.VMEM((2, MB, MB), F32),
            dma((96,)),
            dma((heads,)),
            dma((heads,)),
            dma((blocks,)),
            dma((blocks,)),
            dma((blocks + 2 * groups,)),
            dma((blocks + 2 * groups,)),
            dma((peers + 4,)),
            dma((peers,)),
            dma((peers,)),
            dma((peers,)),
            dma((heads,)),
            dma((heads,)),
            dma((heads // 2,)),
            dma((heads // 2,)),
            dma((heads // 2,)),
            dma((heads // 2,)),
            dma((groups,)),
            dma((groups,)),
            dma((peers,)),
            dma(()),
        ],
        compiler_params=pltpu.CompilerParams(collective_id=0, has_side_effects=True),
        name="layer",
    )(tokens, w_qkv, w_lr, w_out, w_first, w_second, d_out)


def body(tokens, w_qkv, w_lr, w_out, w1_init, w2_init, d_out):
    out, d_tokens, share_first, share_second = layer(
        tokens[0],
        w_qkv,
        w_lr.astype(F32).reshape(-1, HD),
        w_out,
        w1_init[0],
        w2_init[0],
        d_out[0],
    )
    return (out[None], d_tokens[None], share_first.transpose(1, 0)[None], share_second[None])


def solution(mesh):
    placed = (
        P("dp", "seq", "head"),
        P(("seq", "dp"), None, "head"),
        P(None, "head"),
        P(("seq", "dp"), "head"),
        P("head", None, None),
        P("head", None, None),
        P("dp", "seq", "head"),
    )
    return jax.shard_map(
        body,
        mesh=mesh,
        in_specs=placed,
        out_specs=(
            P("dp", "seq", "head"),
            P("dp", "seq", "head"),
            P("head", None, ("seq", "dp")),
            P("head", ("seq", "dp"), None),
        ),
        check_vma=False,
    )
```

```python
import jax
import jax.numpy as jnp
from jax import lax
from jax.experimental import pallas as pl
from jax.experimental.pallas import tpu as pltpu
from jax.sharding import PartitionSpec as P

MB = 64
HD = 128
BF16 = jnp.bfloat16
F32 = jnp.float32
MESH = pl.DeviceIdType.MESH
EPSILON = 1e-06
BASE_RATE = 0.1
GELU_SCALE = 0.7978845608028654
GELU_CUBIC = 0.044715
CONTRACT_LAST = (((1,), (1,)), ((), ()))
CONTRACT_FIRST = (((0,), (0,)), ((), ()))


def matmul(left, right):
    return jnp.dot(left.astype(BF16), right.astype(BF16), preferred_element_type=F32)


def matmul_last(left, right):
    return lax.dot_general(left.astype(BF16), right.astype(BF16), CONTRACT_LAST, preferred_element_type=F32)


def matmul_first(left, right):
    return lax.dot_general(left.astype(BF16), right.astype(BF16), CONTRACT_FIRST, preferred_element_type=F32)


def row_mean(rows):
    return jnp.mean(rows, axis=-1, keepdims=True)


def row_sum(rows):
    return jnp.sum(rows, axis=-1, keepdims=True)


def spread(rates):
    return jnp.concatenate([rates] * 4, axis=1)


def gelu_parts(v, order):
    square = v * v
    bend = jnp.tanh(GELU_SCALE * (v + GELU_CUBIC * square * v))
    tilt = GELU_SCALE * (1.0 + 3.0 * GELU_CUBIC * square)
    flat = 1.0 - bend * bend
    half = 0.5 * v
    value = half * (1.0 + bend)
    slope = 0.5 * (1.0 + bend) + half * flat * tilt
    if order == 1:
        return value, slope
    curve = flat * (tilt + half * (6.0 * GELU_SCALE * GELU_CUBIC) * v - v * bend * tilt * tilt)
    return value, slope, curve


def norm_rows(rows):
    centred = rows - row_mean(rows)
    inv_scale = lax.rsqrt(row_mean(centred * centred) + EPSILON)
    return centred * inv_scale, inv_scale


def layer_kernel(
    tok_ref, wqkv_ref, wlr_ref, wout_ref, w1_ref, w2_ref, dout_ref,
    out_ref, dtok_ref, share1_ref, share2_ref,
    feat, cot, wq, wo, ttt_ref, dproj_ref, dlogit_ref, dw1_ref, dw2_ref,
    send_out, recv_out, pair_send, pair_recv, send_tok, recv_tok, dw_send, dw_recv, dw_sum, share,
    ckt, cqo, s1, s2, w1b, w2b,
    sv_slope, sv_curve, sv_m, sv_x2, sv_narrow,
    qp_xq, qp_dy, qp_wide, qp_g2, qp_dz, qp_ds, qp_kept,
    near_send, feat_recv, cot_recv, wq_recv, wq_recv_low, wo_recv, wo_recv_low,
    chunk_send, chunk_recv, qo_send, qo_recv,
    out_send, out_recv, pair_sends, pair_recvs, tok_send, tok_recv, dw_sems, dw_recvs, share_send, share_recv,
):
    place, head, group = (lax.axis_index(name) for name in ("seq", "head", "dp"))
    count, heads, groups = (lax.axis_size(name) for name in ("seq", "head", "dp"))
    rows = tok_ref.shape[0]
    half = rows // 2
    blocks = count * groups
    barrier = pltpu.get_barrier_semaphore()

    def greet_along(name, mine, size):
        def greet(step, carry):
            peer = lax.rem(mine + step, size)
            pl.semaphore_signal(barrier, inc=1, device_id={name: peer}, device_id_type=MESH)
            return carry

        lax.fori_loop(1, size, greet, 0)

    greet_along("seq", place, count)
    greet_along("head", head, heads)
    greet_along("dp", group, groups)
    pl.semaphore_wait(barrier, count + heads + groups - 3)

    started = []

    def push(src, dst, arrival, device):
        copy = pltpu.make_async_remote_copy(
            src_ref=src,
            dst_ref=dst,
            send_sem=near_send.at[len(started)],
            recv_sem=arrival,
            device_id=device,
            device_id_type=MESH,
        )
        copy.start()
        started.append(tuple(src.shape))

    def arrived(dst, arrival):
        pltpu.make_async_remote_copy(
            src_ref=dst,
            dst_ref=dst,
            send_sem=near_send.at[0],
            recv_sem=arrival,
            device_id={"seq": place},
            device_id_type=MESH,
        ).wait_recv()

    ring = heads // 2
    ring_at, ring_base = lax.rem(head, ring), lax.div(head, ring) * ring
    other_base = ring - ring_base
    partner = {"head": other_base + ring_at}
    ring_up = {"head": ring_base + lax.rem(ring_at + 1, ring)}
    ring_down = {"head": ring_base + lax.rem(ring_at + ring - 1, ring)}

    def ring_push(buffer, arrivals, block, device, src=None):
        push(buffer.at[block] if src is None else src, buffer.at[block], arrivals.at[block], device)

    def ring_start(buffer, arrivals, src):
        ring_push(buffer, arrivals, head, ring_up, src)
        ring_push(buffer, arrivals, head, ring_down, src)

    def ring_partner(buffer, arrivals):
        block = other_base + ring_at
        arrived(buffer.at[block], arrivals.at[block])
        ring_push(buffer, arrivals, block, ring_up)
        ring_push(buffer, arrivals, block, ring_down)

    def ring_step(buffer, arrivals, base, step):
        below = base + lax.rem(ring_at + ring - step, ring)
        arrived(buffer.at[below], arrivals.at[below])
        if step < ring // 2:
            ring_push(buffer, arrivals, below, ring_up)
            above = base + lax.rem(ring_at + step, ring)
            arrived(buffer.at[above], arrivals.at[above])
            if step < ring // 2 - 1:
                ring_push(buffer, arrivals, above, ring_down)

    def feat_step(base, step):
        ring_step(feat, feat_recv, base, step)

    def cot_step(base, step):
        ring_step(cot, cot_recv, base, step)

    sib = place + 1 - 2 * lax.rem(place, 2)
    sibling = {"seq": sib}
    deep = [lax.rem(place + 2 * step, count) for step in range(4)]
    sib_deep = [lax.rem(sib + 2 * step, count) for step in range(4)]
    wide = [lax.rem(group + step, groups) for step in range(4)]
    deep_up, deep_down = {"seq": deep[1]}, {"seq": deep[3]}
    wide_up, wide_down = {"dp": wide[1]}, {"dp": wide[3]}

    def wq_push(block, device, src=None):
        push(wq.at[block] if src is None else src, wq.at[block], wq_recv.at[block], device)

    def wq_relay(from_below, from_above, up, down):
        push(wq.at[from_below, :half], wq.at[from_below, :half], wq_recv.at[from_below], up)
        push(wq.at[from_above, half:], wq.at[from_above, half:], wq_recv_low.at[from_above], down)

    def wq_arrived(block):
        arrived(wq.at[block], wq_recv.at[block])

    def wq_halves_arrived(block):
        arrived(wq.at[block, :half], wq_recv.at[block])
        arrived(wq.at[block, half:], wq_recv_low.at[block])

    def wq_spread(row, src=None):
        block = row * groups + group
        wq_push(block, wide_up, src)
        wq_push(block, wide_down, src)
        wq_push(block, sibling, src)

    def wq_sides(row):
        below, above = row * groups + wide[3], row * groups + wide[1]
        wq_arrived(below)
        wq_arrived(above)
        wq_relay(below, above, wide_up, wide_down)
        wq_push(below, sibling)
        wq_push(above, sibling)

    def wq_far(row):
        block = row * groups + wide[2]
        wq_halves_arrived(block)
        wq_push(block, sibling)

    layers = count // 2

    def halved(number):
        if isinstance(number, int):
            return number // 2, number % 2
        return lax.div(number, 2), lax.rem(number, 2)

    def wo_block(row, column):
        layer, side = halved(row)
        return (side * groups + column) * layers + layer

    def wo_column(row, column):
        return pl.ds((lax.rem(row, 2) * groups + column) * layers, layers)

    def wo_relay(from_below, from_above, up, down):
        push(wo.at[from_below, :half], wo.at[from_below, :half], wo_recv.at[from_below], up)
        push(wo.at[from_above, half:], wo.at[from_above, half:], wo_recv_low.at[from_above], down)

    def wo_column_push(column, device):
        at = wo_column(place, column)
        push(wo.at[at], wo.at[at], wo_recv.at[blocks + lax.rem(place, 2) * groups + column], device)

    def wo_column_arrived(row, column):
        at = wo_column(row, column)
        arrived(wo.at[at], wo_recv.at[blocks + lax.rem(row, 2) * groups + column])

    def wo_sides():
        wo_column_arrived(place, wide[3])
        wo_column_arrived(place, wide[1])
        pair = layers // 2
        low = (lax.rem(place, 2) * groups + wide[3]) * layers
        high = (lax.rem(place, 2) * groups + wide[1]) * layers + pair
        flag = blocks + lax.rem(place, 2) * groups
        push(wo.at[pl.ds(low, pair)], wo.at[pl.ds(low, pair)], wo_recv.at[flag + wide[3]], wide_up)
        push(wo.at[pl.ds(high, pair)], wo.at[pl.ds(high, pair)], wo_recv_low.at[flag + wide[1]], wide_down)
        wo_column_push(wide[3], sibling)
        wo_column_push(wide[1], sibling)

    def wo_far():
        pair = layers // 2
        low = (lax.rem(place, 2) * groups + wide[2]) * layers
        flag = blocks + lax.rem(place, 2) * groups
        arrived(wo.at[pl.ds(low, pair)], wo_recv.at[flag + wide[2]])
        arrived(wo.at[pl.ds(low + pair, pair)], wo_recv_low.at[flag + wide[2]])
        wo_column_push(wide[2], sibling)

    own = place * groups + group
    own_wo = wo_block(place, group)
    ring_start(feat, feat_recv, tok_ref)
    for part in range(3):
        wq[own, :, part * HD : (part + 1) * HD] = wqkv_ref[:, part, :]
    wq_push(own, deep_up)
    wq_push(own, deep_down)
    wq_spread(place)
    feat[head] = tok_ref[...]
    cot[head] = dout_ref[...]
    wo[own_wo] = wout_ref[...]
    feat_step(ring_base, 1)
    ring_push(feat, feat_recv, head, partner, tok_ref)
    wq_sides(place)
    ring_partner(feat, feat_recv)
    feat_step(ring_base, 2)
    for row in (deep[3], deep[1]):
        wq_arrived(row * groups + group)
    wq_relay(deep[3] * groups + group, deep[1] * groups + group, deep_up, deep_down)
    wq_spread(deep[3])
    wq_spread(deep[1])
    push(wout_ref, wo.at[own_wo], wo_recv.at[own_wo], deep_up)
    push(wout_ref, wo.at[own_wo], wo_recv.at[own_wo], deep_down)
    wq_far(place)
    feat_step(other_base, 1)
    feat_step(ring_base, 3)
    feat_step(other_base, 2)
    wq_halves_arrived(deep[2] * groups + group)
    wq_spread(deep[2])
    wq_sides(deep[3])
    wq_sides(deep[1])
    feat_step(ring_base, 4)
    feat_step(other_base, 3)
    ring_start(cot, cot_recv, dout_ref)
    for row in (deep[3], deep[1]):
        arrived(wo.at[wo_block(row, group)], wo_recv.at[wo_block(row, group)])
    wo_relay(wo_block(deep[3], group), wo_block(deep[1], group), deep_up, deep_down)
    wq_sides(deep[2])
    feat_step(other_base, 4)
    wq_far(deep[3])
    wq_far(deep[1])
    cot_step(ring_base, 1)
    wq_far(deep[2])
    far = wo_block(deep[2], group)
    arrived(wo.at[far, :half], wo_recv.at[far])
    arrived(wo.at[far, half:], wo_recv_low.at[far])
    wo_column_push(group, wide_up)
    wo_column_push(group, wide_down)
    wo_column_push(group, sibling)
    for row in sib_deep:
        for column in (0, 1, 3, 2):
            wq_arrived(row * groups + wide[column])

    def depth_rows(buffer, piece):
        both = buffer[pl.ds(2 * piece, 2)]
        return both.reshape(2 * rows, both.shape[-1])

    def out_rows(piece):
        row, column = halved(piece)
        at = wo_block(row, 2 * column)
        return jnp.concatenate([wo[at], wo[at + layers]], axis=0)

    def rate_weights(piece):
        return jnp.concatenate([wlr_ref[pl.ds(2 * piece, 1), :], wlr_ref[pl.ds(2 * piece + 1, 1), :]], axis=1)

    def project(piece, carry):
        total, logit = carry
        part = feat[piece]
        total = total + jnp.dot(part, depth_rows(wq, piece), preferred_element_type=F32)
        weights = jnp.broadcast_to(rate_weights(piece), (HD, 2 * rows)).astype(BF16)
        return total, logit + matmul_last(part, weights)

    projected, logit = lax.fori_loop(
        0, heads, project, (jnp.zeros((rows, 3 * HD), F32), jnp.zeros((rows, HD), F32)), unroll=4
    )
    keys = projected[:, HD : 2 * HD]
    rates = (BASE_RATE / HD) * jax.nn.sigmoid(logit)
    rate_rows = jnp.transpose(rates)[:16, :]
    rate_high = rate_rows.astype(BF16)
    block_rows = ckt.at[place]
    block_rows[:rows, :HD] = keys.astype(BF16)
    block_rows[:rows, HD:] = (projected[:, 2 * HD :] - keys).astype(BF16)
    block_rows[rows:, :HD] = rate_high
    block_rows[rows:, HD:] = (rate_rows - rate_high.astype(F32)).astype(BF16)
    cqo[place, :, :HD] = projected[:, :HD].astype(BF16)

    def chunk_copy(source, to, which):
        return pltpu.make_async_remote_copy(
            src_ref=ckt.at[source],
            dst_ref=ckt.at[source],
            send_sem=chunk_send.at[which],
            recv_sem=chunk_recv.at[source],
            device_id={"seq": to},
            device_id_type=MESH,
        )

    s1[...] = w1_ref[...]
    s2[...] = w2_ref[...]

    def send_chunk():
        chunk_copy(place, deep[1], count).start()
        chunk_copy(place, deep[3], count + 1).start()
        chunk_copy(place, sib, count + 2).start()
        chunk_copy(place, deep[2], count + 3).start()

    @pl.when(place < 4)
    def _():
        send_chunk()

    ring_push(cot, cot_recv, head, partner, dout_ref)

    def same_side(source):
        return jnp.logical_and(source != place, lax.rem(source + place, 2) == 0)

    def take_chunk(source):
        @pl.when(source != place)
        def _():
            chunk_copy(source, place, 0).wait_recv()

        @pl.when(same_side(source))
        def _():
            chunk_copy(source, sib, source).start()

    place_row = lax.broadcasted_iota(jnp.int32, (MB, MB), 0)
    place_col = lax.broadcasted_iota(jnp.int32, (MB, MB), 1)

    def span_of(half_at):
        return slice(half_at * MB, (half_at + 1) * MB)

    def state_block(turn, half_at, e):
        block = 2 * turn + half_at
        k = ckt[turn, span_of(half_at), :HD]
        t = ckt[turn, span_of(half_at), HD:].astype(F32)
        first, second = s1[...].astype(BF16), s2[...].astype(BF16)
        x2, slope, curve = gelu_parts(matmul(k, first), 2)
        n, s = norm_rows(matmul(x2, second))
        r = n - t
        cross = row_mean(r * n)
        h = r - row_mean(r) - n * cross
        g2 = s * h
        m = matmul_last(g2, second)
        kt = jnp.transpose(k)
        x2t = jnp.transpose(x2)
        s1[...] = s1[...] - matmul(kt, spread(e) * (m * slope))
        s2[...] = s2[...] - matmul(x2t, e * g2)
        w1b[block] = first
        w2b[block] = second
        sv_slope[block] = slope
        sv_curve[block] = curve
        sv_m[block] = m
        sv_x2[block] = x2.astype(BF16)
        sv_narrow[block, 0] = n
        sv_narrow[block, 1] = r
        sv_narrow[block, 2] = h
        sv_narrow[block, 3] = g2
        sv_narrow[block, 4] = jnp.broadcast_to(s, (MB, HD))
        sv_narrow[block, 5] = jnp.broadcast_to(cross, (MB, HD))
        sv_narrow[block, 6] = e

    def query_forward(turn, half_at):
        block = 2 * turn + half_at
        span = span_of(half_at)
        q, k = cqo[turn, span, :HD], ckt[turn, span, :HD]
        first, second, x2 = w1b[block], w2b[block], sv_x2[block]
        g1 = (sv_m[block] * sv_slope[block]).astype(BF16)
        g2 = sv_narrow[block, 3].astype(BF16)
        e_row = jnp.transpose(sv_narrow[block, 6])[:MB, :]
        causal = jnp.where(place_col <= place_row, e_row, 0.0)
        raw1 = matmul_last(q, k)
        a1 = raw1 * causal
        xq, slope_q = gelu_parts(matmul(q, first) - matmul(a1, g1), 1)
        raw2 = matmul_last(xq, x2)
        a2 = raw2 * causal
        nq, sq = norm_rows(matmul(xq, second) - matmul(a2, g2))
        return q, first, second, x2, g1, g2, causal, raw1, a1, xq, slope_q, raw2, a2, nq, sq

    def query_part(turn, half_at):
        q, first, second, x2, g1, g2, causal, raw1, a1, xq, slope_q, raw2, a2, nq, sq = query_forward(
            turn, half_at
        )
        do = cqo[turn, span_of(half_at), HD:].astype(F32)
        dyq = (sq * (do - row_mean(do) - nq * row_mean(do * nq))).astype(BF16)
        da2 = -matmul_last(dyq, g2)
        ds2 = (da2 * causal).astype(BF16)
        dzq = ((matmul_last(dyq, second) + matmul(ds2, x2)) * slope_q).astype(BF16)
        da1 = -matmul_last(dzq, g1)
        qp_xq[half_at] = xq.astype(BF16)
        qp_dy[half_at] = dyq
        qp_wide[half_at, 0] = -matmul_first(a1, dzq)
        qp_wide[half_at, 1] = matmul_first(ds2, xq)
        qp_g2[half_at] = -matmul_first(a2, dyq)
        qp_dz[half_at] = dzq
        qp_ds[half_at] = (da1 * causal).astype(BF16)
        qp_kept[half_at] = jnp.where(place_col <= place_row, da2 * raw2 + da1 * raw1, 0.0)

    def chain_block(turn, half_at, mine):
        block = 2 * turn + half_at
        span = span_of(half_at)
        d1, d2 = dw1_ref[...], dw2_ref[...]
        d1b, d2b = d1.astype(BF16), d2.astype(BF16)
        k = ckt[turn, span, :HD]
        first, second, x2 = w1b[block], w2b[block], sv_x2[block]
        slope, curve, m = sv_slope[block], sv_curve[block], sv_m[block]
        n, r, h, g2, s, cross, e = (sv_narrow[block, i] for i in range(7))
        p1 = matmul(k, d1b)
        p2 = matmul_last(x2, d2b)
        dg1 = qp_wide[half_at, 0] - spread(e) * p1
        dmb = (dg1 * slope).astype(BF16)
        dg2 = qp_g2[half_at] - e * p2 + matmul(dmb, second)
        dh = s * dg2
        mean_n = row_mean(dh * n)
        dr = dh - row_mean(dh) - n * mean_n
        dn = dr - cross * dh - r * mean_n
        dy = s * (dn - row_mean(dn) - n * row_mean(dn * n)) - n * (row_mean(dg2 * h) * s * s)
        dyb = dy.astype(BF16)
        dx2 = qp_wide[half_at, 1] - matmul(e * g2, d2b) + matmul_last(dyb, second)
        dz1 = dx2 * slope + dg1 * m * curve
        dz1b = dz1.astype(BF16)
        narrow = jnp.concatenate([g2.astype(BF16), dyb, qp_dy[half_at]], axis=0)
        dw2_ref[...] = d2 + matmul_first(narrow, jnp.concatenate([dmb, x2, qp_xq[half_at]], axis=0))
        inputs = jnp.concatenate([k, cqo[turn, span, :HD]], axis=0)
        dw1_ref[...] = d1 + matmul_first(inputs, jnp.concatenate([dz1b, qp_dz[half_at]], axis=0))
        if mine:
            q, do = cqo[turn, span, :HD], cqo[turn, span, HD:].astype(F32)
            ds1 = qp_ds[half_at]
            dq = do + matmul_last(qp_dz[half_at], first) + matmul(ds1, k)
            g1 = m * slope
            dk = matmul_first(ds1, q) - matmul_last(spread(e) * g1, d1b) + dr + matmul_last(dz1b, first)
            de = row_sum(jnp.transpose(qp_kept[half_at])) - row_sum(p1 * g1) - row_sum(p2 * g2)
            dproj_ref[span, :HD] = dq.astype(BF16)
            dproj_ref[span, HD : 2 * HD] = dk.astype(BF16)
            dproj_ref[span, 2 * HD :] = (-dr).astype(BF16)
            dlogit_ref[span, :] = de * e * (1.0 - e * (HD / BASE_RATE))

    def share_out(step, source):
        to = lax.rem(head + step, heads)
        return pltpu.make_async_remote_copy(
            src_ref=send_out.at[to],
            dst_ref=recv_out.at[source],
            send_sem=out_send.at[to],
            recv_sem=out_recv.at[source],
            device_id={"head": to},
            device_id_type=MESH,
        )

    def send_terms():
        rows_out = ttt_ref[...]
        for step in range(1, heads):
            to = lax.rem(head + step, heads)
            send_out[to] = matmul_last(rows_out, out_rows(to)).astype(BF16)
            if step > 1:
                share_out(step - 1, head).start()
        recv_out[head] = matmul_last(rows_out, out_rows(head)).astype(BF16)
        share_out(heads - 1, head).start()

    def state_turn(turn, carry):
        @pl.when(turn + 2 < count)
        def _():
            take_chunk(turn + 2)

        rate_row = ckt[turn, rows:, :HD].astype(F32) + ckt[turn, rows:, HD:].astype(F32)
        spread_rates = jnp.transpose(jnp.broadcast_to(rate_row[:1, :], (HD, rows)))
        state_block(turn, 0, spread_rates[:MB])
        state_block(turn, 1, spread_rates[MB:])
        return carry

    def early_turn(turn, carry):
        @pl.when(jnp.logical_and(place >= 4, turn == jnp.maximum(place - 5, 0)))
        def _():
            send_chunk()

        state_turn(turn, 0)

        @pl.when(turn == 0)
        def _():
            ring_partner(cot, cot_recv)
            cot_step(ring_base, 2)
            wo_sides()

        @pl.when(turn == 1)
        def _():
            cot_step(other_base, 1)
            cot_step(ring_base, 3)
            wo_far()

        @pl.when(turn == 2)
        def _():
            cot_step(other_base, 2)
            cot_step(ring_base, 4)

        return carry

    def qo_copy(source, to):
        return pltpu.make_async_remote_copy(
            src_ref=cqo.at[source],
            dst_ref=cqo.at[source],
            send_sem=qo_send.at[to],
            recv_sem=qo_recv.at[source],
            device_id={"seq": to},
            device_id_type=MESH,
        )

    def late_turn(turn, carry):
        state_turn(turn, 0)

        @pl.when(turn == jnp.maximum(place, 5))
        def _():
            for half_at in range(2):
                parts = query_forward(place, half_at)
                ttt_ref[span_of(half_at), :] = (parts[0].astype(F32) + parts[-2]).astype(BF16)
            send_terms()

        @pl.when(turn == 3)
        def _():
            cot_step(other_base, 3)

        @pl.when(turn == 4)
        def _():
            cot_step(other_base, 4)
            d_ttt = jnp.zeros((rows, HD), F32)
            for piece in range(heads):
                d_ttt = d_ttt + jnp.dot(cot[piece], out_rows(piece), preferred_element_type=F32)
            cqo[place, :, HD:] = d_ttt.astype(BF16)

            def send_qo(to, carry):
                qo_copy(place, to).start()
                return carry

            lax.fori_loop(0, place, send_qo, 0)

        return carry

    take_chunk(0)
    take_chunk(1)
    lax.fori_loop(0, 3, early_turn, 0)
    for column in range(groups):
        wo_column_arrived(sib, column)
    lax.fori_loop(3, count, late_turn, 0)

    dw1_ref[...] = jnp.zeros_like(dw1_ref)
    dw2_ref[...] = jnp.zeros_like(dw2_ref)

    def take_qo(source):
        @pl.when(source > place)
        def _():
            qo_copy(source, place).wait_recv()

    take_qo(count - 1)
    query_part(count - 1, 1)

    def back_turn(step, carry):
        turn = count - 1 - step
        take_qo(turn - 1)
        chain_block(turn, 1, False)
        query_part(turn, 0)
        chain_block(turn, 0, False)
        query_part(turn - 1, 1)
        return carry

    lax.fori_loop(0, count - 1 - place, back_turn, 0)
    chain_block(place, 1, True)
    query_part(place, 0)
    chain_block(place, 0, True)

    def pair_copy(spot):
        return pltpu.make_async_remote_copy(
            src_ref=pair_send.at[spot],
            dst_ref=pair_recv.at[spot],
            send_sem=pair_sends.at[spot],
            recv_sem=pair_recvs.at[spot],
            device_id=partner,
            device_id_type=MESH,
        )

    def share_tok(spot, source):
        return pltpu.make_async_remote_copy(
            src_ref=send_tok.at[spot],
            dst_ref=recv_tok.at[source],
            send_sem=tok_send.at[spot],
            recv_sem=tok_recv.at[source],
            device_id={"head": ring_base + spot},
            device_id_type=MESH,
        )

    d_proj = dproj_ref[...]
    d_logit = jnp.concatenate([dlogit_ref[...], dlogit_ref[...]], axis=1)

    def token_term(to):
        return matmul_last(d_proj, depth_rows(wq, to)) + d_logit * rate_weights(to)

    spots = [lax.rem(ring_at + step, ring) for step in (4, 3, 5, 2, 6, 1, 7, 0)]
    for at, spot in enumerate(spots):
        pair_send[spot] = token_term(other_base + spot).astype(BF16)
        if at > 0:
            pair_copy(spots[at - 1]).start()
    last_pair = spots[-1]

    def dw_copy(step, source):
        to = lax.rem(group + step, groups)
        return pltpu.make_async_remote_copy(
            src_ref=dw_send.at[to],
            dst_ref=dw_recv.at[source],
            send_sem=dw_sems.at[step],
            recv_sem=dw_recvs.at[source],
            device_id={"dp": to},
            device_id_type=MESH,
        )

    def share_copy(to):
        return pltpu.make_async_remote_copy(
            src_ref=dw_sum.at[to],
            dst_ref=share,
            send_sem=share_send.at[to],
            recv_sem=share_recv,
            device_id={"seq": to},
            device_id_type=MESH,
        )

    @pl.when(place == 0)
    def _():
        joined = jnp.transpose(jnp.concatenate([dw1_ref[...], dw2_ref[...]], axis=0))
        parts = joined.reshape(count, groups, -1, 2 * HD)
        for part in range(groups):
            dw_send[part] = parts[:, part]
        for step in range(1, groups):
            dw_copy(step, group).start()

    for at, spot in enumerate(spots):
        term = token_term(ring_base + spot)
        if at == 0:
            pair_copy(last_pair).start()
        if at > 0:
            share_tok(spots[at - 1], ring_at).start()
        pair_copy(spot).wait_recv()
        term = (term + pair_recv[spot].astype(F32)).astype(BF16)
        if at < ring - 1:
            send_tok[spot] = term
        else:
            recv_tok[ring_at] = term

    @pl.when(place == 0)
    def _():
        total = dw_send[group]
        for step in range(1, groups):
            source = lax.rem(group + step, groups)
            dw_copy(step, source).wait_recv()
            total = total + dw_recv[source]
        dw_sum[...] = total
        share[...] = total[0]
        for to in range(1, count):
            share_copy(to).start()

    def sum_terms(copy, received):
        def add(step, total):
            source = lax.rem(head + step, heads)

            @pl.when(step > 0)
            def _():
                copy(0, source).wait_recv()

            return total + received[source].astype(F32)

        return lax.fori_loop(0, heads, add, jnp.zeros((rows, 2 * HD), F32)).astype(BF16)

    out_ref[...] = sum_terms(share_out, recv_out)
    total = recv_tok[ring_at].astype(F32)
    for step in (1, 7, 2, 6, 3, 5, 4):
        source = lax.rem(ring_at + step, ring)
        share_tok(ring_at, source).wait_recv()
        total = total + recv_tok[source].astype(F32)
    dtok_ref[...] = total.astype(BF16)

    @pl.when(place > 0)
    def _():
        share_copy(0).wait_recv()

    share1_ref[...] = share[:, :HD]
    share2_ref[...] = share[:, HD:]

    @pl.when(place == 0)
    def _():
        for step in range(1, groups):
            dw_copy(step, group).wait_send()
        for to in range(1, count):
            share_copy(to).wait_send()

    for which in range(4):
        chunk_copy(place, sib, count + which).wait_send()

    def sent_chunk(source, carry):
        @pl.when(same_side(source))
        def _():
            chunk_copy(source, sib, source).wait_send()

        return carry

    lax.fori_loop(0, count, sent_chunk, 0)

    def sent_qo(to, carry):
        qo_copy(place, to).wait_send()
        return carry

    lax.fori_loop(0, place, sent_qo, 0)

    def sent_terms(step, carry):
        share_out(step, head).wait_send()
        return carry

    lax.fori_loop(1, heads, sent_terms, 0)
    for spot in spots:
        pair_copy(spot).wait_send()
    for spot in spots[:-1]:
        share_tok(spot, ring_at).wait_send()
    views = [feat.at[0], wq.at[0], wq.at[0, :half], wo.at[0], wo.at[0, :half]]
    views += [wo.at[pl.ds(0, layers)], wo.at[pl.ds(0, layers // 2)]]
    view_of = {tuple(view.shape): view for view in views}
    for index, shape in enumerate(started):
        pltpu.make_async_remote_copy(
            src_ref=view_of[shape],
            dst_ref=view_of[shape],
            send_sem=near_send.at[index],
            recv_sem=feat_recv.at[0],
            device_id={"seq": place},
            device_id_type=MESH,
        ).wait_send()


def layer(tokens, w_qkv, w_lr, w_out, w_first, w_second, d_out):
    rows, width = tokens.shape
    peers, heads, groups = (lax.axis_size(name) for name in ("seq", "head", "dp"))
    inner = w_first.shape[1]
    share = inner // (peers * groups)
    blocks = peers * groups
    steps = peers * (rows // MB)
    vmem = pl.BlockSpec(memory_space=pltpu.VMEM)
    dma = pltpu.SemaphoreType.DMA
    return pl.pallas_call(
        layer_kernel,
        out_shape=(
            jax.ShapeDtypeStruct((rows, width), BF16),
            jax.ShapeDtypeStruct((rows, width), BF16),
            jax.ShapeDtypeStruct((share, HD), F32),
            jax.ShapeDtypeStruct((share, HD), F32),
        ),
        in_specs=[vmem] * 7,
        out_specs=(vmem,) * 4,
        scratch_shapes=[
            pltpu.VMEM((heads, rows, width), BF16),
            pltpu.VMEM((heads, rows, width), BF16),
            pltpu.VMEM((blocks, rows, 3 * HD), BF16),
            pltpu.VMEM((blocks, rows, HD), BF16),
            pltpu.VMEM((rows, HD), BF16),
            pltpu.VMEM((rows, 3 * HD), BF16),
            pltpu.VMEM((rows, HD), F32),
            pltpu.VMEM((HD, inner), F32),
            pltpu.VMEM((HD, inner), F32),
            pltpu.VMEM((heads, rows, width), BF16),
            pltpu.VMEM((heads, rows, width), BF16),
            pltpu.VMEM((heads // 2, rows, width), BF16),
            pltpu.VMEM((heads // 2, rows, width), BF16),
            pltpu.VMEM((heads // 2, rows, width), BF16),
            pltpu.VMEM((heads // 2, rows, width), BF16),
            pltpu.VMEM((groups, peers, share, 2 * HD), F32),
            pltpu.VMEM((groups, peers, share, 2 * HD), F32),
            pltpu.VMEM((peers, share, 2 * HD), F32),
            pltpu.VMEM((share, 2 * HD), F32),
            pltpu.VMEM((peers, rows + 16, 2 * HD), BF16),
            pltpu.VMEM((peers, rows, 2 * HD), BF16),
            pltpu.VMEM((HD, inner), F32),
            pltpu.VMEM((inner, HD), F32),
            pltpu.VMEM((steps, HD, inner), BF16),
            pltpu.VMEM((steps, inner, HD), BF16),
            pltpu.VMEM((steps, MB, inner), F32),
            pltpu.VMEM((steps, MB, inner), F32),
            pltpu.VMEM((steps, MB, inner), F32),
            pltpu.VMEM((steps, MB, inner), BF16),
            pltpu.VMEM((steps, 7, MB, HD), F32),
            pltpu.VMEM((2, MB, inner), BF16),
            pltpu.VMEM((2, MB, HD), BF16),
            pltpu.VMEM((2, 2, MB, inner), F32),
            pltpu.VMEM((2, MB, HD), F32),
            pltpu.VMEM((2, MB, inner), BF16),
            pltpu.VMEM((2, MB, MB), BF16),
            pltpu.VMEM((2, MB, MB), F32),
            dma((96,)),
            dma((heads,)),
            dma((heads,)),
            dma((blocks,)),
            dma((blocks,)),
            dma((blocks + 2 * groups,)),
            dma((blocks + 2 * groups,)),
            dma((peers + 4,)),
            dma((peers,)),
            dma((peers,)),
            dma((peers,)),
            dma((heads,)),
            dma((heads,)),
            dma((heads // 2,)),
            dma((heads // 2,)),
            dma((heads // 2,)),
            dma((heads // 2,)),
            dma((groups,)),
            dma((groups,)),
            dma((peers,)),
            dma(()),
        ],
        compiler_params=pltpu.CompilerParams(collective_id=0, has_side_effects=True),
        name="layer",
    )(tokens, w_qkv, w_lr, w_out, w_first, w_second, d_out)


def body(tokens, w_qkv, w_lr, w_out, w1_init, w2_init, d_out):
    out, d_tokens, share_first, share_second = layer(
        tokens[0],
        w_qkv,
        w_lr.astype(F32).reshape(-1, HD),
        w_out,
        w1_init[0],
        w2_init[0],
        d_out[0],
    )
    return (out[None], d_tokens[None], share_first.transpose(1, 0)[None], share_second[None])


def solution(mesh):
    placed = (
        P("dp", "seq", "head"),
        P(("seq", "dp"), None, "head"),
        P(None, "head"),
        P(("seq", "dp"), "head"),
        P("head", None, None),
        P("head", None, None),
        P("dp", "seq", "head"),
    )
    return jax.shard_map(
        body,
        mesh=mesh,
        in_specs=placed,
        out_specs=(
            P("dp", "seq", "head"),
            P("dp", "seq", "head"),
            P("head", None, ("seq", "dp")),
            P("head", ("seq", "dp"), None),
        ),
        check_vma=False,
    )
```
